512 devices in a mesh: segment: 4 (over x), rep: 8 (over y, core), box: 16 (over z).
Axes of the slice: x: 4, y: 4, z: 16, core: 2. Of those that a mesh axis runs over, the one named last changes fastest.
Arguments:
- centers: float32 [512, 4, 4, 512], P(('rep', 'box')), may hold values from -6 to 6
- box_radii: float32 [512, 4, 4, 512], P(('rep', 'box')), may hold values from 0.001 to 0.01
- labels: int32 [512], P(('rep', 'box')), may hold values from 0 to 9
- certified: int32 [512], P(('rep', 'box')), may hold values from 0 to 1, as said below
- conv_weights: bfloat16 [4, 9, 512, 512], P('segment', None, 'box'), may hold values from -0.01171875 to 0.01171875
- conv_bias: float32 [4, 512], P('segment'), may hold values from -1.2 to 1.2
- head_weight: bfloat16 [512, 10], replicated, may hold values from -0.25 to 0.25
- head_bias: float32 [10], replicated, may hold values from -4 to 4
Outputs:
- lower_bounds: float32 [128, 4, 5], P(('rep', 'box'), 'segment')
The draws below stay inside these ranges and needn't reach their ends.
Inputs may be any that keep to these rules, and one draw needn't show every extreme that they name: `certified`: for each box index and each i, the devices 2i and 2i + 1 along rep hold 4 boxes with value 0 together; in each box index some such pair has all 4 of them on one device.
All inputs are finite; a program needn't handle non-finite values.
Results may differ from the reference program's by a relative error of at most 0.00055.
Values may be sent and summed in bfloat16 or wider, within the bound.
A program may use at most 64 MiB of HBM per device.

```python
import math
import jax
import jax.numpy as jnp
from jax import lax

H = 512
CLASSES = 10
K = 5
SIDE = 4
B_DEV = 4
BOXES = 512
N_SEGMENT = 4
N_REP = 8
N_BOX = 16


def draw_certified(key, part):
    half_dev = B_DEV // 2
    pair_count = N_REP // 2
    count_key, order_key = jax.random.split(key)

    def column_counts(column_key):
        diff_key, pick_key, sign_key = jax.random.split(column_key, 3)
        offsets = jax.random.randint(diff_key, (pair_count,), -half_dev, half_dev + 1)
        chosen = jax.random.randint(pick_key, (), 0, pair_count)
        flip = 2 * jax.random.randint(sign_key, (), 0, 2) - 1
        offsets = jnp.where(jnp.arange(pair_count) == chosen, flip * half_dev, offsets)
        paired = jnp.stack([half_dev + offsets, half_dev - offsets], axis=1).reshape(N_REP)
        return paired.astype(jnp.int32)
    counts = jax.vmap(column_counts)(jax.random.split(count_key, N_BOX)).T
    ranking = jax.vmap(lambda block_key: jax.random.permutation(block_key, B_DEV))(jax.random.split(order_key, N_REP * N_BOX))
    ranking = ranking.reshape(N_REP, N_BOX, B_DEV)
    return (ranking >= counts[:, :, None]).astype(jnp.int32).reshape(N_REP * N_BOX * B_DEV)


def touch_ends(drawn, stream_key, least, largest):
    shape = drawn.shape
    place = [jax.random.randint(jax.random.fold_in(stream_key, axis), (), 0, shape[axis]) for axis in range(len(shape))]
    drawn = drawn.at[tuple(place)].set(least)
    longest = shape.index(max(shape))
    place[longest] = (place[longest] + 1) % shape[longest]
    return drawn.at[tuple(place)].set(largest)


def block_scale(key, dims, cuts, low, top_value):
    def one(dim, blocks):
        draws = jax.random.uniform(jax.random.fold_in(jax.random.fold_in(key, 6), dim), (blocks,), jnp.float32, low / len(cuts), top_value / len(cuts))
        return jnp.repeat(jnp.exp(draws), dims[dim] // blocks).reshape((-1,) + (1,) * (len(dims) - dim - 1))

    gain = one(*cuts[0])
    for cut in cuts[1:]:
        gain = gain * one(*cut)
    return gain


def bell_draw(own_key, dims, scale, bound, pieces=(), kind=jnp.bfloat16):
    values = jax.random.normal(own_key, dims, jnp.float32) * scale
    if len(pieces) > 0:
        values = block_scale(own_key, dims, pieces, -0.22, 0.18) * values
    return jnp.clip(values, min=-bound, max=bound).astype(kind)


def setup_inputs(seed: int = 0) -> dict:
    key_list = jax.random.split(jax.random.key(seed), 9)
    centers = bell_draw(key_list[0], (BOXES, SIDE, SIDE, H), 1.0, 6.0, ((0, 128),), jnp.float32)
    box_radii = jnp.clip(jnp.exp(math.log(0.01) - 2.30258502 * jax.random.uniform(key_list[1], (BOXES, SIDE, SIDE, H), jnp.float32) ** block_scale(key_list[1], (BOXES, SIDE, SIDE, H), ((0, 128),), -0.2, 0.2)), 0.001, 0.01)
    labels = touch_ends(jax.random.randint(key_list[2], (BOXES,), 0, CLASSES), jax.random.fold_in(key_list[2], 1), 0, CLASSES - 1).astype(jnp.int32)
    certified = draw_certified(jax.random.fold_in(key_list[8], 71), 0)
    conv_weights = bell_draw(key_list[4], (N_SEGMENT, 9, H, H), (64 * 9 * H) ** -0.5, 0.01171875, ((0, 4), (2, 16)))
    conv_bias = bell_draw(key_list[5], (N_SEGMENT, H), 0.2, 1.2, ((0, 4),), jnp.float32)
    head_weight = bell_draw(key_list[6], (H, CLASSES), H ** -0.5, 0.25)
    head_bias = bell_draw(key_list[7], (CLASSES,), 1.0, 4.0, (), jnp.float32)
    return {"centers": centers, "box_radii": box_radii, "labels": labels, "certified": certified, "conv_weights": conv_weights, "conv_bias": conv_bias, "head_weight": head_weight, "head_bias": head_bias}


def convolve(values, kernel):
    extent = values.shape[1]
    padded = jnp.pad(values, ((0, 0), (1, 1), (1, 1), (0, 0)))
    result = jnp.zeros(values.shape[:3] + (kernel.shape[1],), jnp.float32)
    for tap_index in range(9):
        row_shift, col_shift = divmod(tap_index, 3)
        window = padded[:, row_shift:row_shift + extent, col_shift:col_shift + extent, :]
        result = result + lax.dot_general(window, kernel[tap_index], (((3,), (1,)), ((), ())), preferred_element_type=jnp.float32)
    return result


def convolve_back(gradient, kernel):
    extent = gradient.shape[1]
    padded_sum = jnp.zeros((gradient.shape[0], extent + 2, extent + 2, kernel.shape[2]), jnp.float32)
    for tap_index in range(9):
        row_shift, col_shift = divmod(tap_index, 3)
        product = lax.dot_general(gradient, kernel[tap_index], (((3,), (0,)), ((), ())), preferred_element_type=jnp.float32)
        padded_sum = padded_sum.at[:, row_shift:row_shift + extent, col_shift:col_shift + extent, :].add(product)
    return padded_sum[:, 1:extent + 1, 1:extent + 1, :]


def forward_layer(middle, radius, kernel, magnitude, shift_bias):
    centre = convolve(middle.astype(jnp.bfloat16), kernel) + shift_bias
    spread = convolve(radius.astype(jnp.bfloat16), magnitude)
    lower_edge = centre - spread
    upper_edge = centre + spread
    upper_pos = jax.nn.relu(upper_edge)
    lower_neg = jax.nn.relu(-lower_edge)
    lower_pos = jax.nn.relu(lower_edge)
    slope_now = upper_pos / (upper_pos + lower_neg)
    intercept = slope_now * lower_neg
    middle = middle + 0.5 * (upper_pos + lower_pos)
    radius = radius + 0.5 * (upper_pos - lower_pos)
    return middle, radius, slope_now, intercept


def backward_layer(coeffs, slope_now, intercept, kernel, shift_bias):
    scaled = coeffs * slope_now[:, None]
    layer_term = jnp.sum(scaled * shift_bias + jnp.minimum(coeffs, 0.0) * intercept[:, None], axis=(2, 3, 4))
    gradient = scaled.astype(jnp.bfloat16).reshape((-1,) + scaled.shape[2:])
    coeffs = coeffs + convolve_back(gradient, kernel).reshape(coeffs.shape)
    return coeffs, layer_term


def head_coeffs(label_box, head_weight, head_bias, extent, channels):
    classes = head_bias.shape[0]
    spec_rows = jnp.arange(K, dtype=jnp.int32)[None, :]
    others = (label_box[:, None] + 1 + spec_rows) % classes
    class_ids = jnp.arange(classes, dtype=jnp.int32)
    selector = (class_ids[None, None, :] == label_box[:, None, None]).astype(jnp.float32) - (class_ids[None, None, :] == others[:, :, None]).astype(jnp.float32)
    pooled = jnp.einsum("bkc,fc->bkf", selector, head_weight.astype(jnp.float32), precision=lax.Precision.HIGHEST) / float(extent * extent)
    offset = jnp.einsum("bkc,c->bk", selector, head_bias, precision=lax.Precision.HIGHEST)
    coeffs = jnp.broadcast_to(pooled[:, :, None, None, :], (label_box.shape[0], K, extent, extent, channels))
    return coeffs, offset


def concretize(coeffs, centre_box, radius_box):
    return jnp.sum(coeffs * centre_box[:, None] - jnp.abs(coeffs) * radius_box[:, None], axis=(2, 3, 4))


def reference(centers, box_radii, labels, certified, conv_weights, conv_bias, head_weight, head_bias):
    groups = N_REP * N_BOX
    magnitude = jnp.abs(conv_weights)
    shape_box = (groups, B_DEV, SIDE, SIDE, H)

    def one_group(inputs):
        centre_box, radius_box, label_box = inputs
        middle, radius = centre_box, radius_box
        slopes, intercepts = [], []
        for layer_index in range(N_SEGMENT):
            middle, radius, slope_now, intercept = forward_layer(middle, radius, conv_weights[layer_index], magnitude[layer_index], conv_bias[layer_index])
            slopes.append(slope_now)
            intercepts.append(intercept)
        coeffs, bound_sum = head_coeffs(label_box, head_weight, head_bias, SIDE, H)
        for layer_index in reversed(range(N_SEGMENT)):
            if layer_index < N_SEGMENT - 1:
                coeffs = lax.optimization_barrier(coeffs.astype(jnp.bfloat16)).astype(jnp.float32)
            coeffs, layer_term = backward_layer(coeffs, slopes[layer_index], intercepts[layer_index], conv_weights[layer_index], conv_bias[layer_index])
            bound_sum = bound_sum + layer_term
        return bound_sum + concretize(coeffs, centre_box, radius_box)

    bounds = lax.map(one_group, (centers.reshape(shape_box), box_radii.reshape(shape_box), labels.reshape(groups, B_DEV)))
    alive_rows = (1 - certified).reshape(groups, B_DEV).astype(jnp.float32)
    return bounds * alive_rows[:, :, None]
```

```python
import functools

import jax
import jax.numpy as jnp
from jax import lax
from jax.experimental import pallas as pl
from jax.experimental.pallas import tpu as pltpu
from jax.sharding import PartitionSpec as P

K = 5
CHUNKS = 3
TAPS = 9
bf16 = jnp.bfloat16
f32 = jnp.float32
MESH = pl.DeviceIdType.MESH


def kernel(
    n_seg, n_rep, n_box, classes,
    cert, lab, cen, rad, cw, bias, hw, hb, out,
    W, S, L, G, C8, R8, PT, MID, fin, fout, cin, cout, CF, slope, cept, HC, HO, T,
    loc, zs, zr, ys, yr, cs, cr, xs, xr, fs, fr, bs, br, ts, tr,
):
    s = lax.axis_index("segment")
    r = lax.axis_index("rep")
    z = lax.axis_index("box")
    c = lax.rem(r, 2)
    par = lax.rem(r // 2, 2)
    mate = {"rep": r + 1 - 2 * c}
    y_up = {"rep": lax.rem(r + 2, n_rep)}
    y_down = {"rep": lax.rem(r + n_rep - 2, n_rep)}
    z_up = {"box": lax.rem(z + 1, n_box)}
    z_down = {"box": lax.rem(z + n_box - 1, n_box)}
    peers = []
    for dx in range(n_seg):
        for dc in range(2):
            if dx or dc:
                peers.append(
                    {"segment": lax.rem(s + dx, n_seg), "rep": r + dc * (1 - 2 * c)}
                )
    shard = W.shape[1] // n_box
    half = shard // 2
    lanes = W.shape[2] // 2
    per = TAPS // CHUNKS
    last_up = n_box // 2
    last_down = n_box - 1 - last_up

    own = pltpu.make_async_copy(
        cw.at[0], W.at[:, pl.ds(pl.multiple_of(z * shard, shard), shard), :], loc.at[0]
    )
    own.start()
    own_c = pltpu.make_async_copy(cen, C8.at[pl.ds(4 * c, 4)], loc.at[1])
    own_c.start()
    own_r = pltpu.make_async_copy(rad, R8.at[pl.ds(4 * c, 4)], loc.at[2])
    own_r.start()

    barrier = pltpu.get_barrier_semaphore()
    near = [y_up, y_down, z_up, z_down] + peers
    for device in near:
        pl.semaphore_signal(barrier, inc=1, device_id=device, device_id_type=MESH)
    pl.semaphore_wait(barrier, len(near))

    def remote(src, dst, send, recv, device):
        return pltpu.make_async_remote_copy(
            src_ref=src, dst_ref=dst, send_sem=send, recv_sem=recv,
            device_id=device, device_id_type=MESH,
        )

    def piece(b, core, side, j=None):
        row = pl.multiple_of(b * shard + core * half, half)
        lane = pl.multiple_of(side * lanes, lanes)
        taps = pl.ds(0, TAPS) if j is None else pl.ds(j * per, per)
        return W.at[taps, pl.ds(row, half), pl.ds(lane, lanes)]

    def source(d, k):
        if d == 0:
            return lax.rem(z + n_box - k, n_box)
        return lax.rem(z + k, n_box)

    def z_copy(d, k, j):
        ref = piece(source(d, k - 1), c, par, j)
        return remote(ref, ref, zs.at[d, k - 1, j], zr.at[d, k - 1, j], (z_up, z_down)[d])

    def z_land(d, k, j):
        ref = piece(source(d, k), c, par, j)
        remote(ref, ref, zs.at[d, k - 1, j], zr.at[d, k - 1, j], (z_up, z_down)[d]).wait_recv()

    def y_copy(d, k, j):
        ref = piece(source(d, k), c, par, j)
        return remote(ref, ref, ys.at[d, k - 1, j], yr.at[d, k - 1, j], (y_up, y_down)[d])

    def y_land(d, k, j):
        ref = piece(source(d, k), c, 1 - par, j)
        remote(ref, ref, ys.at[d, k - 1, j], yr.at[d, k - 1, j], (y_up, y_down)[d]).wait_recv()

    def c_copy(d, k, h):
        ref = piece(source(d, k), c, par if h == 0 else 1 - par)
        return remote(ref, ref, cs.at[d, k - 1, h], cr.at[d, k - 1, h], mate)

    def c_land(d, k, h):
        ref = piece(source(d, k), 1 - c, par if h == 0 else 1 - par)
        remote(ref, ref, cs.at[d, k - 1, h], cr.at[d, k - 1, h], mate).wait_recv()

    own.wait()
    for j in range(CHUNKS):
        z_copy(0, 1, j).start()
        z_copy(1, 1, j).start()

    own_c.wait()
    own_r.wait()
    pair_c = remote(C8.at[pl.ds(4 * c, 4)], C8.at[pl.ds(4 * c, 4)], xs.at[0], xr.at[0], mate)
    pair_r = remote(R8.at[pl.ds(4 * c, 4)], R8.at[pl.ds(4 * c, 4)], xs.at[1], xr.at[1], mate)
    row8 = lax.broadcasted_iota(jnp.int32, (8, 128), 0)
    lane8 = lax.broadcasted_iota(jnp.int32, (8, 128), 1)
    tile = jnp.zeros((8, 128), f32)
    for i in range(4):
        alive_i = (1 - cert[i]).astype(f32)
        label_i = lab[i].astype(f32)
        here = lane8 == 4 * c + i
        tile = jnp.where(here & (row8 == 0), alive_i, tile)
        tile = jnp.where(here & (row8 == 1), label_i, tile)
    PT[c] = tile
    pair_t = remote(PT.at[c], PT.at[c], xs.at[2], xr.at[2], mate)
    pair_t.start()
    pair_c.start()
    pair_r.start()

    p_row = lax.broadcasted_iota(jnp.int32, (80, 128), 0)
    p_col = lax.broadcasted_iota(jnp.int32, (80, 128), 1)
    same = (p_row // 16) == (p_col // 16)
    dy = lax.rem(p_col, 16) // 4 - lax.rem(p_row, 16) // 4
    dx_ = lax.rem(p_col, 4) - lax.rem(p_row, 4)
    for t in range(TAPS):
        a, b = divmod(t, 3)
        S[t] = jnp.where(same & (dy == a - 1) & (dx_ == b - 1), 1.0, 0.0).astype(bf16)
    G[...] = jnp.zeros_like(G)

    def gather_step(k, _):
        for d in range(2):
            for j in range(CHUNKS):
                z_land(d, k, j)
                go_on = k < (last_up, last_down)[d]

                @pl.when(go_on)
                def _():
                    z_copy(d, k + 1, j).start()

                y_copy(d, k, j).start()
            c_copy(d, k, 0).start()

        @pl.when(k > 1)
        def _():
            for d in range(2):
                for j in range(CHUNKS):
                    y_land(d, k - 1, j)
                c_copy(d, k - 1, 1).start()

        return 0

    lax.fori_loop(1, last_down + 1, gather_step, 0)
    if last_up > last_down:
        for j in range(CHUNKS):
            z_land(0, last_up, j)
            y_copy(0, last_up, j).start()
        c_copy(0, last_up, 0).start()
    for d in range(2):
        for j in range(CHUNKS):
            y_land(d, last_down, j)
        c_copy(d, last_down, 1).start()
    if last_up > last_down:
        for j in range(CHUNKS):
            y_land(0, last_up, j)
        c_copy(0, last_up, 1).start()

    remote(PT.at[1 - c], PT.at[1 - c], xs.at[2], xr.at[2], mate).wait_recv()
    other = pl.ds(4 * (1 - c), 4)
    remote(C8.at[other], C8.at[other], xs.at[0], xr.at[0], mate).wait_recv()
    remote(R8.at[other], R8.at[other], xs.at[1], xr.at[1], mate).wait_recv()
    both = PT[0] + PT[1]
    alive_row = both[0:1, :]
    label_row = both[1:2, :]
    alive = jnp.sum(jnp.where(lane8 == row8, alive_row, 0.0), axis=1, keepdims=True)
    labels = jnp.sum(jnp.where(lane8 == row8, label_row, 0.0), axis=1, keepdims=True)
    rank = jnp.sum(jnp.where(lane8 < row8, alive_row, 0.0), axis=1, keepdims=True)
    live_no = jnp.where(alive > 0.5, rank, -1.0)
    first = (2 * c).astype(f32)

    @pl.when(s == 0)
    def _():
        for m in range(2):
            pick = jnp.where(live_no == first + m, 1.0, 0.0)
            middle = jnp.zeros((16, C8.shape[3]), f32)
            radius = jnp.zeros((16, C8.shape[3]), f32)
            for i in range(8):
                take = pick[i : i + 1, :] > 0.5
                middle = jnp.where(take, C8[i].reshape(middle.shape), middle)
                radius = jnp.where(take, R8[i].reshape(radius.shape), radius)
            MID[16 * m : 16 * m + 16] = middle
            MID[32 + 16 * m : 48 + 16 * m] = radius

    @pl.when(s == n_seg - 1)
    def _():
        row = lax.broadcasted_iota(jnp.int32, (16, 1), 0)
        spec = lax.rem(row, 8).astype(f32)
        lab0 = jnp.sum(jnp.where(live_no == first, labels, 0.0), axis=0, keepdims=True)
        lab1 = jnp.sum(jnp.where(live_no == first + 1.0, labels, 0.0), axis=0, keepdims=True)
        true = jnp.where(row < 8, lab0, lab1)
        rival = true + 1.0 + spec
        rival = jnp.where(rival >= classes, rival - classes, rival)
        ids = lax.broadcasted_iota(jnp.int32, (16, classes), 1).astype(f32)
        selector = jnp.where(ids == true, 1.0, 0.0) - jnp.where(ids == rival, 1.0, 0.0)
        selector = jnp.where(spec < K, selector, 0.0)
        pooled = lax.dot_general(
            selector.astype(bf16), hw[...], (((1,), (1,)), ((), ())), preferred_element_type=f32
        ) / 16.0
        HC[...] = pooled.reshape(2, 8, pooled.shape[1])
        offset = jnp.sum(selector * hb[...], axis=1, keepdims=True)
        lane16 = lax.broadcasted_iota(jnp.int32, (16, 128), 1)
        HO[...] = jnp.where(lane16 == 0, offset, 0.0)

    for d in range(2):
        for k in range(1, (last_up, last_down)[d] + 1):
            for h in range(2):
                c_land(d, k, h)

    @pl.when(s > 0)
    def _():
        remote(fout, fin, fs, fr, {"segment": lax.rem(s + 1, n_seg)}).wait_recv()
        MID[...] = fin[...].astype(f32)

    G[0:64] = MID[...].astype(bf16)
    for t in range(TAPS):
        L[t, 0:64] = jnp.dot(
            S[t, 0:64], G[...], preferred_element_type=f32
        ).astype(bf16)
    rows_in = (((1,), (1,)), ((), ()))
    centre = jnp.zeros((32, W.shape[1]), f32)
    spread = jnp.zeros((32, W.shape[1]), f32)
    for t in range(TAPS):
        w = W[t]
        centre += lax.dot_general(L[t, 0:32], w, rows_in, preferred_element_type=f32)
        spread += lax.dot_general(
            L[t, 32:64], jnp.abs(w), rows_in, preferred_element_type=f32
        )
    centre = centre + bias[...]
    low = centre - spread
    up = centre + spread
    up_pos = jnp.maximum(up, 0.0)
    low_pos = jnp.maximum(low, 0.0)
    low_neg = jnp.maximum(-low, 0.0)
    fout[0:32] = (MID[0:32] + 0.5 * (up_pos + low_pos)).astype(bf16)
    fout[32:64] = (MID[32:64] + 0.5 * (up_pos - low_pos)).astype(bf16)

    @pl.when(s < n_seg - 1)
    def _():
        remote(fout, fin, fs, fr, {"segment": lax.rem(s + 1, n_seg)}).start()

    slope_now = up_pos / (up_pos + low_neg)
    cept_now = slope_now * low_neg
    slope[...] = slope_now.reshape(slope.shape)
    cept[...] = cept_now.reshape(cept.shape)

    slot = s * 2 + c
    down_x = {"segment": lax.rem(s + n_seg - 1, n_seg)}
    for m in range(2):
        @pl.when(s == n_seg - 1)
        def _():
            for k in range(K):
                CF[16 * k : 16 * k + 16] = jnp.broadcast_to(
                    HC[m, k : k + 1], (16, HC.shape[2])
                )

        @pl.when(s < n_seg - 1)
        def _():
            remote(cout.at[m], cin.at[m], bs.at[m], br.at[m], down_x).wait_recv()
            CF[...] = cin[m].astype(f32)

        slope_m = slope[m]
        for k in range(K):
            G[16 * k : 16 * k + 16] = (CF[16 * k : 16 * k + 16] * slope_m).astype(bf16)
        for t in range(TAPS):
            L[t] = jnp.dot(S[TAPS - 1 - t], G[...], preferred_element_type=f32).astype(bf16)
        new = CF[...]
        for t in range(TAPS):
            new += jnp.dot(L[t], W[t], preferred_element_type=f32)

        @pl.when(s > 0)
        def _():
            cout[m] = new.astype(bf16)
            remote(cout.at[m], cin.at[m], bs.at[m], br.at[m], down_x).start()

        cept_m = cept[m]
        first_section = s == 0
        for k in range(K):
            now = CF[16 * k : 16 * k + 16]
            part = now * slope_m * bias[...] + jnp.minimum(now, 0.0) * cept_m
            new_k = new[16 * k : 16 * k + 16]
            ends = new_k * MID[16 * m : 16 * m + 16] - jnp.abs(new_k) * MID[
                32 + 16 * m : 48 + 16 * m
            ]
            part = part + jnp.where(first_section, ends, 0.0)
            part = jnp.sum(part, axis=0, keepdims=True)
            folded = part[:, 0:128]
            for q in range(1, part.shape[1] // 128):
                folded = folded + part[:, 128 * q : 128 * q + 128]
            at = 8 * m + k
            folded = folded + jnp.where(s == n_seg - 1, HO[at : at + 1, :], 0.0)
            T[slot, at : at + 1, :] = folded

    sends = []
    for n, device in enumerate(peers):
        copy = remote(T.at[slot], T.at[slot], ts.at[n], tr.at[slot], device)
        copy.start()
        sends.append(copy)
    for dx in range(n_seg):
        for dc in range(2):
            if dx or dc:
                there = lax.rem(s + dx, n_seg) * 2 + c + dc * (1 - 2 * c)
                remote(T.at[there], T.at[there], ts.at[0], tr.at[there], mate).wait_recv()
    mine = jnp.where(row8[:, 0:1] == 4 * c + s, live_no, -1.0)
    mine = jnp.max(mine, axis=0, keepdims=True)
    total = jnp.zeros((8, 128), f32)
    for core in range(2):
        for m in range(2):
            part = T[core, 8 * m : 8 * m + 8]
            for x in range(1, n_seg):
                part = part + T[2 * x + core, 8 * m : 8 * m + 8]
            total = jnp.where((mine == float(2 * core + m)) & (row8 < K), part, total)
    column = jnp.sum(total, axis=1, keepdims=True)
    line = jnp.sum(jnp.where(row8 == lane8, column, 0.0), axis=0, keepdims=True)
    out[0] = line[:, 0:K]

    for copy in sends:
        copy.wait_send()

    def drain(k, _):
        for d in range(2):
            for j in range(CHUNKS):
                z_copy(d, k, j).wait_send()
                y_copy(d, k, j).wait_send()
            for h in range(2):
                c_copy(d, k, h).wait_send()
        return 0

    lax.fori_loop(1, last_down + 1, drain, 0)
    if last_up > last_down:
        for j in range(CHUNKS):
            z_copy(0, last_up, j).wait_send()
            y_copy(0, last_up, j).wait_send()
        for h in range(2):
            c_copy(0, last_up, h).wait_send()
    pair_c.wait_send()
    pair_r.wait_send()
    pair_t.wait_send()

    @pl.when(s < n_seg - 1)
    def _():
        remote(fout, fin, fs, fr, {"segment": lax.rem(s + 1, n_seg)}).wait_send()

    @pl.when(s > 0)
    def _():
        for m in range(2):
            remote(cout.at[m], cin.at[m], bs.at[m], br.at[m], down_x).wait_send()


def per_device(mesh_shape, centers, box_radii, labels, certified, conv_weights, conv_bias,
               head_weight, head_bias):
    n_seg, n_rep, n_box = (mesh_shape[a] for a in ("segment", "rep", "box"))
    h = conv_weights.shape[-1]
    classes = head_bias.shape[0]
    steps = n_box // 2
    dma = pltpu.SemaphoreType.DMA
    vmem = pl.BlockSpec(memory_space=pltpu.VMEM)
    smem = pl.BlockSpec(memory_space=pltpu.SMEM)
    hbm = pl.BlockSpec(memory_space=pl.ANY)
    return pl.pallas_call(
        functools.partial(kernel, n_seg, n_rep, n_box, classes),
        out_shape=jax.ShapeDtypeStruct((1, 1, K), f32),
        in_specs=[smem, smem, hbm, hbm, hbm, vmem, vmem, vmem],
        out_specs=vmem,
        scratch_shapes=[
            pltpu.VMEM((TAPS, h, h), bf16),
            pltpu.VMEM((TAPS, 80, 128), bf16),
            pltpu.VMEM((TAPS, 80, h), bf16),
            pltpu.VMEM((128, h), bf16),
            pltpu.VMEM((8, 4, 4, h), f32),
            pltpu.VMEM((8, 4, 4, h), f32),
            pltpu.VMEM((2, 8, 128), f32),
            pltpu.VMEM((64, h), f32),
            pltpu.VMEM((64, h), bf16),
            pltpu.VMEM((64, h), bf16),
            pltpu.VMEM((2, 80, h), bf16),
            pltpu.VMEM((2, 80, h), bf16),
            pltpu.VMEM((80, h), f32),
            pltpu.VMEM((2, 16, h), f32),
            pltpu.VMEM((2, 16, h), f32),
            pltpu.VMEM((2, 8, h), f32),
            pltpu.VMEM((16, 128), f32),
            pltpu.VMEM((2 * n_seg, 16, 128), f32),
            dma((3,)),
            dma((2, steps, CHUNKS)),
            dma((2, steps, CHUNKS)),
            dma((2, steps, CHUNKS)),
            dma((2, steps, CHUNKS)),
            dma((2, steps, 2)),
            dma((2, steps, 2)),
            dma((3,)),
            dma((3,)),
            dma,
            dma,
            dma((2,)),
            dma((2,)),
            dma((2 * n_seg,)),
            dma((2 * n_seg,)),
        ],
        compiler_params=pltpu.CompilerParams(collective_id=0, has_side_effects=True),
    )(certified, labels, centers, box_radii, conv_weights, conv_bias, head_weight,
      head_bias[None, :])


def solution(mesh):
    placed = (
        P(("rep", "box"), None, None, None),
        P(("rep", "box"), None, None, None),
        P(("rep", "box")),
        P(("rep", "box")),
        P("segment", None, "box", None),
        P("segment", None),
        P(),
        P(),
    )
    return jax.shard_map(
        functools.partial(per_device, dict(mesh.shape)),
        mesh=mesh,
        in_specs=placed,
        out_specs=P(("rep", "box"), "segment", None),
        check_vma=False,
    )
```

```python
import functools

import jax
import jax.numpy as jnp
from jax import lax
from jax.experimental import pallas as pl
from jax.experimental.pallas import tpu as pltpu
from jax.sharding import PartitionSpec as P

K = 5
TAPS = 9
TREE = (
    (1, 0), (-1, 0), (3, 0), (-3, 0),
    (2, 3), (-2, -3), (4, 3), (-4, -3), (6, 3), (-6, -3),
    (5, 6), (-5, -6), (7, 6), (-7, -6), (8, 6),
)
FIRST = (1, -1, 3, -3)
HALVED = 0
LAG = 5
LAG2 = 9
bf16 = jnp.bfloat16
f32 = jnp.float32
MESH = pl.DeviceIdType.MESH


def kernel(
    n_seg, n_rep, n_box, classes,
    cert_in, lab_in, cen, rad, cw, bias_in, hw_in, hb_in, out,
    cert, lab, bias, hw, hb, W, S, L, G, C8, R8, PT, MID, fin, fout, cin, cout, CF, NEW, slope, cept, HC, HO, T,
    loc, zs, zr, ys, yr, cs, cr, xs, xr, fs, fr, bs, br, ts, tr,
):
    s = lax.axis_index("segment")
    r = lax.axis_index("rep")
    z = lax.axis_index("box")
    c = lax.rem(r, 2)
    par = lax.rem(r // 2, 2)
    mate = {"rep": r + 1 - 2 * c}
    y_up = {"rep": lax.rem(r + 2, n_rep)}
    y_down = {"rep": lax.rem(r + n_rep - 2, n_rep)}
    jumps = sorted({o - p for o, p in TREE} | {p - o for o, p in TREE})

    def along(o):
        return {"box": lax.rem(z + n_box + o, n_box)}

    peers = []
    for dx in range(n_seg):
        for dc in range(2):
            if dx or dc:
                peers.append(
                    {"segment": lax.rem(s + dx, n_seg), "rep": r + dc * (1 - 2 * c)}
                )
    shard = W.shape[1] // n_box
    half = shard // 2
    rows_y = n_rep // 2
    y = r // 2
    wide = W.shape[2] // 2
    slim = W.shape[2] // rows_y
    mid_tap = HALVED + (TAPS - HALVED) // 2

    own = pltpu.make_async_copy(
        cw.at[0], W.at[:, pl.ds(pl.multiple_of(z * shard, shard), shard), :], loc.at[0]
    )
    own.start()
    own_c = pltpu.make_async_copy(cen, C8.at[pl.ds(4 * c, 4)], loc.at[1])
    own_c.start()
    own_r = pltpu.make_async_copy(rad, R8.at[pl.ds(4 * c, 4)], loc.at[2])
    own_r.start()
    small = []
    for n, (there, here) in enumerate(
        ((cert_in, cert), (lab_in, lab), (bias_in, bias), (hw_in, hw), (hb_in, hb))
    ):
        copy = pltpu.make_async_copy(there, here, loc.at[3 + n])
        copy.start()
        small.append(copy)

    barrier = pltpu.get_barrier_semaphore()
    near = [y_up, y_down] + [along(o) for o in jumps] + peers
    for device in near:
        pl.semaphore_signal(barrier, inc=1, device_id=device, device_id_type=MESH)
    pl.semaphore_wait(barrier, len(near))

    def remote(src, dst, send, recv, device):
        return pltpu.make_async_remote_copy(
            src_ref=src, dst_ref=dst, send_sem=send, recv_sem=recv,
            device_id=device, device_id_type=MESH,
        )

    def piece(n, core, taps, lane, width, back=0):
        b = lax.rem(z + 2 * n_box - TREE[n][0] + back, n_box)
        row = pl.multiple_of(b * shard + core * half, half)
        lane = pl.multiple_of(lane, width)
        return W.at[pl.ds(taps[0], taps[1] - taps[0]), pl.ds(row, half), pl.ds(lane, width)]

    halved, quartered = (0, HALVED), (HALVED, TAPS)
    low_part, high_part = (HALVED, mid_tap), (mid_tap, TAPS)
    y_next, y_prev = lax.rem(y + 1, rows_y), lax.rem(y + rows_y - 1, rows_y)
    y_far = lax.rem(y + 2, rows_y)

    def z_copies(n, arriving=False):
        offset, parent = TREE[n]
        back = 0 if arriving else offset - parent
        out = []
        if HALVED > 0:
            ref = piece(n, c, halved, par * wide, wide, back)
            out.append(remote(ref, ref, zs.at[n, 0], zr.at[n, 0], along(offset - parent)))
        if HALVED < TAPS:
            ref = piece(n, c, quartered, y * slim, slim, back)
            out.append(remote(ref, ref, zs.at[n, 1], zr.at[n, 1], along(offset - parent)))
        return out

    def y_copies(n, arriving=False):
        out = []
        if HALVED > 0:
            side = 1 - par if arriving else par
            ref = piece(n, c, halved, side * wide, wide)
            out.append(remote(ref, ref, ys.at[n, 0], yr.at[n, 0], (y_up, y_down)[n % 2]))
        if HALVED < TAPS:
            for d in range(2):
                part = (y_prev, y_next)[d] if arriving else y
                ref = piece(n, c, quartered, part * slim, slim)
                out.append(remote(ref, ref, ys.at[n, 1 + d], yr.at[n, 1 + d], (y_up, y_down)[d]))
        return out

    def relay_copies(n, arriving=False):
        out = []
        if HALVED < TAPS:
            for d in range(2):
                part = y_far if arriving else (y_prev, y_next)[d]
                ref = piece(n, c, (low_part, high_part)[d], part * slim, slim)
                out.append(remote(ref, ref, ys.at[n, 3 + d], yr.at[n, 3 + d], (y_up, y_down)[d]))
        return out

    def c_copy(n, arriving=False):
        ref = piece(n, 1 - c if arriving else c, (0, TAPS), 0, 2 * wide)
        return remote(ref, ref, cs.at[n], cr.at[n], mate)

    own.wait()
    index = {offset: n for n, (offset, _) in enumerate(TREE)}
    for offset in FIRST:
        for copy in z_copies(index[offset]):
            copy.start()

    own_c.wait()
    own_r.wait()
    for copy in small:
        copy.wait()
    pair_c = remote(C8.at[pl.ds(4 * c, 4)], C8.at[pl.ds(4 * c, 4)], xs.at[0], xr.at[0], mate)
    pair_r = remote(R8.at[pl.ds(4 * c, 4)], R8.at[pl.ds(4 * c, 4)], xs.at[1], xr.at[1], mate)
    row8 = lax.broadcasted_iota(jnp.int32, (8, 128), 0)
    lane8 = lax.broadcasted_iota(jnp.int32, (8, 128), 1)
    tile = jnp.zeros((8, 128), f32)
    for i in range(4):
        alive_i = (1 - cert[i]).astype(f32)
        label_i = lab[i].astype(f32)
        here = lane8 == 4 * c + i
        tile = jnp.where(here & (row8 == 0), alive_i, tile)
        tile = jnp.where(here & (row8 == 1), label_i, tile)
    PT[c] = tile
    pair_t = remote(PT.at[c], PT.at[c], xs.at[2], xr.at[2], mate)
    pair_t.start()
    pair_c.start()
    pair_r.start()

    p_row = lax.broadcasted_iota(jnp.int32, (80, 128), 0)
    p_col = lax.broadcasted_iota(jnp.int32, (80, 128), 1)
    same = (p_row // 16) == (p_col // 16)
    dy = lax.rem(p_col, 16) // 4 - lax.rem(p_row, 16) // 4
    dx_ = lax.rem(p_col, 4) - lax.rem(p_row, 4)
    for t in range(TAPS):
        a, b = divmod(t, 3)
        S[t] = jnp.where(same & (dy == a - 1) & (dx_ == b - 1), 1.0, 0.0).astype(bf16)
    G[...] = jnp.zeros_like(G)

    def take_y(n):
        for copy in y_copies(n, True):
            copy.wait_recv()
        for copy in relay_copies(n):
            copy.start()

    def take_relayed(n):
        for copy in relay_copies(n, True):
            copy.wait_recv()
        c_copy(n).start()

    count = len(TREE)
    for n in range(count + LAG2):
        if n < count:
            for copy in z_copies(n, True):
                copy.wait_recv()
            for child, (_, parent) in enumerate(TREE):
                if parent == TREE[n][0]:
                    for copy in z_copies(child):
                        copy.start()
            for copy in y_copies(n):
                copy.start()
        if 0 <= n - LAG < count:
            take_y(n - LAG)
        if n >= LAG2:
            take_relayed(n - LAG2)

    remote(PT.at[1 - c], PT.at[1 - c], xs.at[2], xr.at[2], mate).wait_recv()
    other = pl.ds(4 * (1 - c), 4)
    remote(C8.at[other], C8.at[other], xs.at[0], xr.at[0], mate).wait_recv()
    remote(R8.at[other], R8.at[other], xs.at[1], xr.at[1], mate).wait_recv()
    both = PT[0] + PT[1]
    alive_row = both[0:1, :]
    label_row = both[1:2, :]
    alive = jnp.sum(jnp.where(lane8 == row8, alive_row, 0.0), axis=1, keepdims=True)
    labels = jnp.sum(jnp.where(lane8 == row8, label_row, 0.0), axis=1, keepdims=True)
    rank = jnp.sum(jnp.where(lane8 < row8, alive_row, 0.0), axis=1, keepdims=True)
    live_no = jnp.where(alive > 0.5, rank, -1.0)
    first = (2 * c).astype(f32)

    @pl.when(s == 0)
    def _():
        for m in range(2):
            pick = jnp.where(live_no == first + m, 1.0, 0.0)
            middle = jnp.zeros((16, C8.shape[3]), f32)
            radius = jnp.zeros((16, C8.shape[3]), f32)
            for i in range(8):
                take = pick[i : i + 1, :] > 0.5
                middle = jnp.where(take, C8[i].reshape(middle.shape), middle)
                radius = jnp.where(take, R8[i].reshape(radius.shape), radius)
            MID[16 * m : 16 * m + 16] = middle
            MID[32 + 16 * m : 48 + 16 * m] = radius

    @pl.when(s == n_seg - 1)
    def _():
        row = lax.broadcasted_iota(jnp.int32, (16, 1), 0)
        spec = lax.rem(row, 8).astype(f32)
        lab0 = jnp.sum(jnp.where(live_no == first, labels, 0.0), axis=0, keepdims=True)
        lab1 = jnp.sum(jnp.where(live_no == first + 1.0, labels, 0.0), axis=0, keepdims=True)
        true = jnp.where(row < 8, lab0, lab1)
        rival = true + 1.0 + spec
        rival = jnp.where(rival >= classes, rival - classes, rival)
        ids = lax.broadcasted_iota(jnp.int32, (16, classes), 1).astype(f32)
        selector = jnp.where(ids == true, 1.0, 0.0) - jnp.where(ids == rival, 1.0, 0.0)
        selector = jnp.where(spec < K, selector, 0.0)
        pooled = lax.dot_general(
            selector.astype(bf16), hw[...], (((1,), (0,)), ((), ())), preferred_element_type=f32
        ) / 16.0
        HC[...] = pooled.reshape(2, 8, pooled.shape[1])
        offset = jnp.sum(selector * hb[...], axis=1, keepdims=True)
        lane16 = lax.broadcasted_iota(jnp.int32, (16, 128), 1)
        HO[...] = jnp.where(lane16 == 0, offset, 0.0)

    for n in range(count):
        c_copy(n, True).wait_recv()

    up_x = {"segment": lax.rem(s + 1, n_seg)}
    down_x = {"segment": lax.rem(s + n_seg - 1, n_seg)}
    part_h = W.shape[1] // 2
    cols = [slice(h * part_h, (h + 1) * part_h) for h in range(2)]

    def f_copy(h):
        return remote(fout.at[h], fin.at[h], fs.at[h], fr.at[h], up_x)

    def b_copy(m, h):
        return remote(cout.at[m, h], cin.at[m, h], bs.at[m, h], br.at[m, h], down_x)

    rows_in = (((1,), (1,)), ((), ()))
    centre = [jnp.zeros((32, part_h), f32) for _ in range(2)]
    spread = [jnp.zeros((32, part_h), f32) for _ in range(2)]
    for h in range(2):
        @pl.when(s > 0)
        def _():
            f_copy(h).wait_recv()
            MID[:, cols[h]] = fin[h].astype(f32)

        G[0:64, cols[h]] = MID[:, cols[h]].astype(bf16)
        for t in range(TAPS):
            L[t, 0:64, cols[h]] = jnp.dot(
                S[t, 0:64], G[:, cols[h]], preferred_element_type=f32
            ).astype(bf16)
        for n in range(2):
            for t in range(TAPS):
                w = W[t, cols[n], cols[h]]
                centre[n] += lax.dot_general(
                    L[t, 0:32, cols[h]], w, rows_in, preferred_element_type=f32
                )
                spread[n] += lax.dot_general(
                    L[t, 32:64, cols[h]], jnp.abs(w), rows_in, preferred_element_type=f32
                )
            if h == 0:
                continue
            middle_n = centre[n] + bias[:, cols[n]]
            low = middle_n - spread[n]
            up = middle_n + spread[n]
            up_pos = jnp.maximum(up, 0.0)
            low_pos = jnp.maximum(low, 0.0)
            low_neg = jnp.maximum(-low, 0.0)
            fout[n, 0:32] = (MID[0:32, cols[n]] + 0.5 * (up_pos + low_pos)).astype(bf16)
            fout[n, 32:64] = (MID[32:64, cols[n]] + 0.5 * (up_pos - low_pos)).astype(bf16)

            @pl.when(s < n_seg - 1)
            def _():
                f_copy(n).start()

            slope_now = up_pos / (up_pos + low_neg)
            cept_now = slope_now * low_neg
            for m in range(2):
                slope[m, :, cols[n]] = slope_now[16 * m : 16 * m + 16]
                cept[m, :, cols[n]] = cept_now[16 * m : 16 * m + 16]

    slot = s * 2 + c
    for m in range(2):
        for h in range(2):
            @pl.when(s == n_seg - 1)
            def _():
                for k in range(K):
                    CF[16 * k : 16 * k + 16, cols[h]] = jnp.broadcast_to(
                        HC[m, k : k + 1, cols[h]], (16, part_h)
                    )

            @pl.when(s < n_seg - 1)
            def _():
                b_copy(m, h).wait_recv()
                CF[:, cols[h]] = cin[m, h].astype(f32)

            slope_m = slope[m, :, cols[h]]
            for k in range(K):
                rows = slice(16 * k, 16 * k + 16)
                G[rows, cols[h]] = (CF[rows, cols[h]] * slope_m).astype(bf16)
            for t in range(TAPS):
                L[t, :, cols[h]] = jnp.dot(
                    S[TAPS - 1 - t], G[:, cols[h]], preferred_element_type=f32
                ).astype(bf16)
            for n in range(2):
                new = NEW[:, cols[n]] if h else jnp.zeros((80, part_h), f32)
                for t in range(TAPS):
                    new += jnp.dot(
                        L[t, :, cols[h]], W[t, cols[h], cols[n]], preferred_element_type=f32
                    )
                if h == 0:
                    NEW[:, cols[n]] = new
                    continue
                new = new + CF[:, cols[n]]
                NEW[:, cols[n]] = new

                @pl.when(s > 0)
                def _():
                    cout[m, n] = new.astype(bf16)
                    b_copy(m, n).start()

        first_section = s == 0
        for k in range(K):
            rows = slice(16 * k, 16 * k + 16)
            now = CF[rows]
            part = now * slope[m] * bias[...] + jnp.minimum(now, 0.0) * cept[m]
            new_k = NEW[rows]
            ends = new_k * MID[16 * m : 16 * m + 16] - jnp.abs(new_k) * MID[
                32 + 16 * m : 48 + 16 * m
            ]
            part = part + jnp.where(first_section, ends, 0.0)
            part = jnp.sum(part, axis=0, keepdims=True)
            folded = part[:, 0:128]
            for q in range(1, part.shape[1] // 128):
                folded = folded + part[:, 128 * q : 128 * q + 128]
            at = 8 * m + k
            folded = folded + jnp.where(s == n_seg - 1, HO[at : at + 1, :], 0.0)
            T[slot, at : at + 1, :] = folded

    sends = []
    for n, device in enumerate(peers):
        copy = remote(T.at[slot], T.at[slot], ts.at[n], tr.at[slot], device)
        copy.start()
        sends.append(copy)
    for dx in range(n_seg):
        for dc in range(2):
            if dx or dc:
                there = lax.rem(s + dx, n_seg) * 2 + c + dc * (1 - 2 * c)
                remote(T.at[there], T.at[there], ts.at[0], tr.at[there], mate).wait_recv()
    mine = jnp.where(row8[:, 0:1] == 4 * c + s, live_no, -1.0)
    mine = jnp.max(mine, axis=0, keepdims=True)
    total = jnp.zeros((8, 128), f32)
    for core in range(2):
        for m in range(2):
            part = T[core, 8 * m : 8 * m + 8]
            for x in range(1, n_seg):
                part = part + T[2 * x + core, 8 * m : 8 * m + 8]
            total = jnp.where((mine == float(2 * core + m)) & (row8 < K), part, total)
    column = jnp.sum(total, axis=1, keepdims=True)
    line = jnp.sum(jnp.where(row8 == lane8, column, 0.0), axis=0, keepdims=True)
    out[0] = line[:, 0:K]

    for copy in sends:
        copy.wait_send()

    for n in range(count):
        for copy in z_copies(n) + y_copies(n) + relay_copies(n):
            copy.wait_send()
        c_copy(n).wait_send()
    pair_c.wait_send()
    pair_r.wait_send()
    pair_t.wait_send()

    @pl.when(s < n_seg - 1)
    def _():
        for h in range(2):
            f_copy(h).wait_send()

    @pl.when(s > 0)
    def _():
        for m in range(2):
            for h in range(2):
                b_copy(m, h).wait_send()


def per_device(mesh_shape, centers, box_radii, labels, certified, conv_weights, conv_bias,
               head_weight, head_bias):
    n_seg, n_rep, n_box = (mesh_shape[a] for a in ("segment", "rep", "box"))
    h = conv_weights.shape[-1]
    classes = head_bias.shape[0]
    dma = pltpu.SemaphoreType.DMA
    vmem = pl.BlockSpec(memory_space=pltpu.VMEM)
    hbm = pl.BlockSpec(memory_space=pl.ANY)
    return pl.pallas_call(
        functools.partial(kernel, n_seg, n_rep, n_box, classes),
        out_shape=jax.ShapeDtypeStruct((1, 1, K), f32),
        in_specs=[hbm] * 8,
        out_specs=vmem,
        scratch_shapes=[
            pltpu.SMEM(certified.shape, jnp.int32),
            pltpu.SMEM(labels.shape, jnp.int32),
            pltpu.VMEM(conv_bias.shape, f32),
            pltpu.VMEM((classes, h), bf16),
            pltpu.VMEM((1, classes), f32),
            pltpu.VMEM((TAPS, h, h), bf16),
            pltpu.VMEM((TAPS, 80, 128), bf16),
            pltpu.VMEM((TAPS, 80, h), bf16),
            pltpu.VMEM((128, h), bf16),
            pltpu.VMEM((8, 4, 4, h), f32),
            pltpu.VMEM((8, 4, 4, h), f32),
            pltpu.VMEM((2, 8, 128), f32),
            pltpu.VMEM((64, h), f32),
            pltpu.VMEM((2, 64, h // 2), bf16),
            pltpu.VMEM((2, 64, h // 2), bf16),
            pltpu.VMEM((2, 2, 80, h // 2), bf16),
            pltpu.VMEM((2, 2, 80, h // 2), bf16),
            pltpu.VMEM((80, h), f32),
            pltpu.VMEM((80, h), f32),
            pltpu.VMEM((2, 16, h), f32),
            pltpu.VMEM((2, 16, h), f32),
            pltpu.VMEM((2, 8, h), f32),
            pltpu.VMEM((16, 128), f32),
            pltpu.VMEM((2 * n_seg, 16, 128), f32),
            dma((8,)),
            dma((len(TREE), 2)),
            dma((len(TREE), 2)),
            dma((len(TREE), 5)),
            dma((len(TREE), 5)),
            dma((len(TREE),)),
            dma((len(TREE),)),
            dma((3,)),
            dma((3,)),
            dma((2,)),
            dma((2,)),
            dma((2, 2)),
            dma((2, 2)),
            dma((2 * n_seg,)),
            dma((2 * n_seg,)),
        ],
        compiler_params=pltpu.CompilerParams(collective_id=0, has_side_effects=True),
    )(certified, labels, centers, box_radii, conv_weights, conv_bias, head_weight.T,
      head_bias[None, :])


def solution(mesh):
    placed = (
        P(("rep", "box"), None, None, None),
        P(("rep", "box"), None, None, None),
        P(("rep", "box")),
        P(("rep", "box")),
        P("segment", None, "box", None),
        P("segment", None),
        P(),
        P(),
    )
    return jax.shard_map(
        functools.partial(per_device, dict(mesh.shape)),
        mesh=mesh,
        in_specs=placed,
        out_specs=P(("rep", "box"), "segment", None),
        check_vma=False,
    )
```

```python
import functools

import jax
import jax.numpy as jnp
from jax import lax
from jax.experimental import pallas as pl
from jax.experimental.pallas import tpu as pltpu
from jax.sharding import PartitionSpec as P

K = 5
TAPS = 9
TREE = (
    (1, 0), (-1, 0), (2, 0), (-2, 0),
    (3, 2), (-3, -2), (4, 2), (-4, -2), (5, 4), (-5, -4), (6, 4), (-6, -4),
    (7, 6), (-7, -6), (8, 6),
)
FIRST = (1, -1, 2, -2)
LAG = 5
LAG2 = 9
bf16 = jnp.bfloat16
f32 = jnp.float32
MESH = pl.DeviceIdType.MESH


def kernel(
    n_seg, n_rep, n_box, classes,
    cert_in, lab_in, cen, rad, cw, bias_in, hw_in, hb_in, out,
    cert, lab, bias, hw, hb, W, S, L, G, C8, R8, PT, MID, fin, fout, cin, cout, CF, NEW, ACC, slope, cept, HC, HO, T,
    loc, zs, zr, ys, yr, cs, cr, xs, xr, fs, fr, bs, br, ts, tr,
):
    s = lax.axis_index("segment")
    r = lax.axis_index("rep")
    z = lax.axis_index("box")
    c = lax.rem(r, 2)
    mate = {"rep": r + 1 - 2 * c}
    y_up = {"rep": lax.rem(r + 2, n_rep)}
    y_down = {"rep": lax.rem(r + n_rep - 2, n_rep)}
    jumps = sorted({o - p for o, p in TREE} | {p - o for o, p in TREE})

    def along(o):
        return {"box": lax.rem(z + n_box + o, n_box)}

    peers = []
    for dx in range(n_seg):
        for dc in range(2):
            if dx or dc:
                peers.append(
                    {"segment": lax.rem(s + dx, n_seg), "rep": r + dc * (1 - 2 * c)}
                )
    shard = W.shape[1] // n_box
    half = shard // 2
    rows_y = n_rep // 2
    y = r // 2
    wide = W.shape[2] // 2
    slim = W.shape[2] // rows_y
    mid_tap = TAPS // 2

    own = pltpu.make_async_copy(
        cw.at[0], W.at[:, pl.ds(pl.multiple_of(z * shard, shard), shard), :], loc.at[0]
    )
    own.start()
    own_c = pltpu.make_async_copy(cen, C8.at[pl.ds(4 * c, 4)], loc.at[1])
    own_c.start()
    own_r = pltpu.make_async_copy(rad, R8.at[pl.ds(4 * c, 4)], loc.at[2])
    own_r.start()
    small = []
    for n, (there, here) in enumerate(
        ((cert_in, cert), (lab_in, lab), (bias_in, bias), (hw_in, hw), (hb_in, hb))
    ):
        copy = pltpu.make_async_copy(there, here, loc.at[3 + n])
        copy.start()
        small.append(copy)

    barrier = pltpu.get_barrier_semaphore()
    near = [y_up, y_down] + [along(o) for o in jumps] + peers
    for device in near:
        pl.semaphore_signal(barrier, inc=1, device_id=device, device_id_type=MESH)
    pl.semaphore_wait(barrier, len(near))

    def remote(src, dst, send, recv, device):
        return pltpu.make_async_remote_copy(
            src_ref=src, dst_ref=dst, send_sem=send, recv_sem=recv,
            device_id=device, device_id_type=MESH,
        )

    def piece(n, core, taps, lane, width, back=0):
        b = lax.rem(z + 2 * n_box - TREE[n][0] + back, n_box)
        row = pl.multiple_of(b * shard + core * half, half)
        lane = pl.multiple_of(lane, width)
        return W.at[pl.ds(taps[0], taps[1] - taps[0]), pl.ds(row, half), pl.ds(lane, width)]

    every, low_part, high_part = (0, TAPS), (0, mid_tap), (mid_tap, TAPS)
    y_next, y_prev = lax.rem(y + 1, rows_y), lax.rem(y + rows_y - 1, rows_y)
    y_far = lax.rem(y + 2, rows_y)

    def z_copy(n, arriving=False):
        offset, parent = TREE[n]
        ref = piece(n, c, every, y * slim, slim, 0 if arriving else offset - parent)
        return remote(ref, ref, zs.at[n], zr.at[n], along(offset - parent))

    def y_copies(n, arriving=False):
        out = []
        for d in range(2):
            part = (y_prev, y_next)[d] if arriving else y
            ref = piece(n, c, every, part * slim, slim)
            out.append(remote(ref, ref, ys.at[n, d], yr.at[n, d], (y_up, y_down)[d]))
        return out

    def relay_copies(n, arriving=False):
        out = []
        for d in range(2):
            part = y_far if arriving else (y_prev, y_next)[d]
            ref = piece(n, c, (low_part, high_part)[d], part * slim, slim)
            out.append(remote(ref, ref, ys.at[n, 2 + d], yr.at[n, 2 + d], (y_up, y_down)[d]))
        return out

    near_half = y // 2

    def c_copy(n, far, arriving=False):
        side = 1 - near_half if far else near_half
        ref = piece(n, 1 - c if arriving else c, every, side * wide, wide)
        return remote(ref, ref, cs.at[n, far], cr.at[n, far], mate)

    own.wait()
    index = {offset: n for n, (offset, _) in enumerate(TREE)}
    for offset in FIRST:
        z_copy(index[offset]).start()

    own_c.wait()
    own_r.wait()
    for copy in small:
        copy.wait()
    pair_c = remote(C8.at[pl.ds(4 * c, 4)], C8.at[pl.ds(4 * c, 4)], xs.at[0], xr.at[0], mate)
    pair_r = remote(R8.at[pl.ds(4 * c, 4)], R8.at[pl.ds(4 * c, 4)], xs.at[1], xr.at[1], mate)
    row8 = lax.broadcasted_iota(jnp.int32, (8, 128), 0)
    lane8 = lax.broadcasted_iota(jnp.int32, (8, 128), 1)
    tile = jnp.zeros((8, 128), f32)
    for i in range(4):
        alive_i = (1 - cert[i]).astype(f32)
        label_i = lab[i].astype(f32)
        here = lane8 == 4 * c + i
        tile = jnp.where(here & (row8 == 0), alive_i, tile)
        tile = jnp.where(here & (row8 == 1), label_i, tile)
    PT[c] = tile
    pair_t = remote(PT.at[c], PT.at[c], xs.at[2], xr.at[2], mate)
    pair_t.start()
    pair_c.start()
    pair_r.start()

    p_row = lax.broadcasted_iota(jnp.int32, (80, 128), 0)
    p_col = lax.broadcasted_iota(jnp.int32, (80, 128), 1)
    same = (p_row // 16) == (p_col // 16)
    dy = lax.rem(p_col, 16) // 4 - lax.rem(p_row, 16) // 4
    dx_ = lax.rem(p_col, 4) - lax.rem(p_row, 4)
    for t in range(TAPS):
        a, b = divmod(t, 3)
        S[t] = jnp.where(same & (dy == a - 1) & (dx_ == b - 1), 1.0, 0.0).astype(bf16)
    G[...] = jnp.zeros_like(G)

    count = len(TREE)

    def take_relayed(n):
        for copy in relay_copies(n, True):
            copy.wait_recv()
        c_copy(n, 1).start()

    for n in range(count + LAG):
        if n < count:
            z_copy(n, True).wait_recv()
            for child, (_, parent) in enumerate(TREE):
                if parent == TREE[n][0]:
                    z_copy(child).start()
            for copy in y_copies(n):
                copy.start()
        if n >= LAG:
            for copy in y_copies(n - LAG, True):
                copy.wait_recv()
            for copy in relay_copies(n - LAG):
                copy.start()
            c_copy(n - LAG, 0).start()
        if n >= LAG2:
            take_relayed(n - LAG2)

    remote(PT.at[1 - c], PT.at[1 - c], xs.at[2], xr.at[2], mate).wait_recv()
    other = pl.ds(4 * (1 - c), 4)
    remote(C8.at[other], C8.at[other], xs.at[0], xr.at[0], mate).wait_recv()
    remote(R8.at[other], R8.at[other], xs.at[1], xr.at[1], mate).wait_recv()
    both = PT[0] + PT[1]
    alive_row = both[0:1, :]
    label_row = both[1:2, :]
    alive = jnp.sum(jnp.where(lane8 == row8, alive_row, 0.0), axis=1, keepdims=True)
    labels = jnp.sum(jnp.where(lane8 == row8, label_row, 0.0), axis=1, keepdims=True)
    rank = jnp.sum(jnp.where(lane8 < row8, alive_row, 0.0), axis=1, keepdims=True)
    live_no = jnp.where(alive > 0.5, rank, -1.0)
    first = (2 * c).astype(f32)

    @pl.when(s == 0)
    def _():
        for m in range(2):
            pick = jnp.where(live_no == first + m, 1.0, 0.0)
            middle = jnp.zeros((16, C8.shape[3]), f32)
            radius = jnp.zeros((16, C8.shape[3]), f32)
            for i in range(8):
                take = pick[i : i + 1, :] > 0.5
                middle = jnp.where(take, C8[i].reshape(middle.shape), middle)
                radius = jnp.where(take, R8[i].reshape(radius.shape), radius)
            MID[16 * m : 16 * m + 16] = middle
            MID[32 + 16 * m : 48 + 16 * m] = radius

    @pl.when(s == n_seg - 1)
    def _():
        row = lax.broadcasted_iota(jnp.int32, (16, 1), 0)
        spec = lax.rem(row, 8).astype(f32)
        lab0 = jnp.sum(jnp.where(live_no == first, labels, 0.0), axis=0, keepdims=True)
        lab1 = jnp.sum(jnp.where(live_no == first + 1.0, labels, 0.0), axis=0, keepdims=True)
        true = jnp.where(row < 8, lab0, lab1)
        rival = true + 1.0 + spec
        rival = jnp.where(rival >= classes, rival - classes, rival)
        ids = lax.broadcasted_iota(jnp.int32, (16, classes), 1).astype(f32)
        selector = jnp.where(ids == true, 1.0, 0.0) - jnp.where(ids == rival, 1.0, 0.0)
        selector = jnp.where(spec < K, selector, 0.0)
        pooled = lax.dot_general(
            selector.astype(bf16), hw[...], (((1,), (0,)), ((), ())), preferred_element_type=f32
        ) / 16.0
        HC[...] = pooled.reshape(2, 8, pooled.shape[1])
        offset = jnp.sum(selector * hb[...], axis=1, keepdims=True)
        lane16 = lax.broadcasted_iota(jnp.int32, (16, 128), 1)
        HO[...] = jnp.where(lane16 == 0, offset, 0.0)

    up_x = {"segment": lax.rem(s + 1, n_seg)}
    down_x = {"segment": lax.rem(s + n_seg - 1, n_seg)}
    part_h = W.shape[1] // 2
    cols = [slice(h * part_h, (h + 1) * part_h) for h in range(2)]
    rows_in = (((1,), (1,)), ((), ()))

    def f_copy(h):
        return remote(fout.at[h], fin.at[h], fs.at[h], fr.at[h], up_x)

    def b_copy(m, h):
        return remote(cout.at[m, h], cin.at[m, h], bs.at[m, h], br.at[m, h], down_x)

    def half_forward(h, finish):
        here = pl.ds(pl.multiple_of(h * part_h, part_h), part_h)
        G[0:64, here] = MID[:, here].astype(bf16)
        for t in range(TAPS):
            L[t, 0:64, here] = jnp.dot(
                S[t, 0:64], G[:, here], preferred_element_type=f32
            ).astype(bf16)
        for n in range(2):
            start = ACC[n] if finish else jnp.zeros((64, part_h), f32)
            centre, spread = start[0:32], start[32:64]
            for t in range(TAPS):
                w = W[t, cols[n], here]
                centre += lax.dot_general(
                    L[t, 0:32, here], w, rows_in, preferred_element_type=f32
                )
                spread += lax.dot_general(
                    L[t, 32:64, here], jnp.abs(w), rows_in, preferred_element_type=f32
                )
            if not finish:
                ACC[n, 0:32] = centre
                ACC[n, 32:64] = spread
                continue
            centre = centre + bias[:, cols[n]]
            low = centre - spread
            up = centre + spread
            up_pos = jnp.maximum(up, 0.0)
            low_pos = jnp.maximum(low, 0.0)
            low_neg = jnp.maximum(-low, 0.0)
            fout[n, 0:32] = (MID[0:32, cols[n]] + 0.5 * (up_pos + low_pos)).astype(bf16)
            fout[n, 32:64] = (MID[32:64, cols[n]] + 0.5 * (up_pos - low_pos)).astype(bf16)

            @pl.when(s < n_seg - 1)
            def _():
                f_copy(n).start()

            slope_now = up_pos / (up_pos + low_neg)
            cept_now = slope_now * low_neg
            for m in range(2):
                slope[m, :, cols[n]] = slope_now[16 * m : 16 * m + 16]
                cept[m, :, cols[n]] = cept_now[16 * m : 16 * m + 16]

    for n in range(count):
        c_copy(n, 0, True).wait_recv()

    @pl.when(s == 0)
    def _():
        half_forward(near_half, False)

    for n in range(count + LAG - LAG2, count):
        take_relayed(n)
    for n in range(count):
        c_copy(n, 1, True).wait_recv()

    @pl.when(s > 0)
    def _():
        f_copy(0).wait_recv()
        MID[:, cols[0]] = fin[0].astype(f32)
        half_forward(0, False)
        f_copy(1).wait_recv()
        MID[:, cols[1]] = fin[1].astype(f32)

    half_forward(jnp.where(s == 0, 1 - near_half, 1), True)

    slot = s * 2 + c

    def terms(m):
        for k in range(K):
            rows = slice(16 * k, 16 * k + 16)
            now = CF[m, rows]
            part = now * slope[m] * bias[...] + jnp.minimum(now, 0.0) * cept[m]
            new_k = NEW[m, rows]
            ends = new_k * MID[16 * m : 16 * m + 16] - jnp.abs(new_k) * MID[
                32 + 16 * m : 48 + 16 * m
            ]
            part = part + jnp.where(s == 0, ends, 0.0)
            part = jnp.sum(part, axis=0, keepdims=True)
            folded = part[:, 0:128]
            for q in range(1, part.shape[1] // 128):
                folded = folded + part[:, 128 * q : 128 * q + 128]
            at = 8 * m + k
            folded = folded + jnp.where(s == n_seg - 1, HO[at : at + 1, :], 0.0)
            T[slot, at : at + 1, :] = folded

    for m in range(2):
        for h in range(2):
            @pl.when(s == n_seg - 1)
            def _():
                for k in range(K):
                    CF[m, 16 * k : 16 * k + 16, cols[h]] = jnp.broadcast_to(
                        HC[m, k : k + 1, cols[h]], (16, part_h)
                    )

            @pl.when(s < n_seg - 1)
            def _():
                b_copy(m, h).wait_recv()
                CF[m, :, cols[h]] = cin[m, h].astype(f32)

            slope_m = slope[m, :, cols[h]]
            for k in range(K):
                rows = slice(16 * k, 16 * k + 16)
                G[rows, cols[h]] = (CF[m, rows, cols[h]] * slope_m).astype(bf16)
            for t in range(TAPS):
                L[t, :, cols[h]] = jnp.dot(
                    S[TAPS - 1 - t], G[:, cols[h]], preferred_element_type=f32
                ).astype(bf16)
            for n in range(2):
                new = NEW[m, :, cols[n]] if h else jnp.zeros((80, part_h), f32)
                for t in range(TAPS):
                    new += jnp.dot(
                        L[t, :, cols[h]], W[t, cols[h], cols[n]], preferred_element_type=f32
                    )
                if h == 0:
                    NEW[m, :, cols[n]] = new
                    continue
                new = new + CF[m, :, cols[n]]
                NEW[m, :, cols[n]] = new

                @pl.when(s > 0)
                def _():
                    cout[m, n] = new.astype(bf16)
                    b_copy(m, n).start()

        if m == 0:
            pl.when(s == 0)(functools.partial(terms, 0))

    pl.when(s > 0)(functools.partial(terms, 0))
    terms(1)

    sends = []
    for n, device in enumerate(peers):
        copy = remote(T.at[slot], T.at[slot], ts.at[n], tr.at[slot], device)
        copy.start()
        sends.append(copy)
    for dx in range(n_seg):
        for dc in range(2):
            if dx or dc:
                there = lax.rem(s + dx, n_seg) * 2 + c + dc * (1 - 2 * c)
                remote(T.at[there], T.at[there], ts.at[0], tr.at[there], mate).wait_recv()
    mine = jnp.where(row8[:, 0:1] == 4 * c + s, live_no, -1.0)
    mine = jnp.max(mine, axis=0, keepdims=True)
    total = jnp.zeros((8, 128), f32)
    for core in range(2):
        for m in range(2):
            part = T[core, 8 * m : 8 * m + 8]
            for x in range(1, n_seg):
                part = part + T[2 * x + core, 8 * m : 8 * m + 8]
            total = jnp.where((mine == float(2 * core + m)) & (row8 < K), part, total)
    column = jnp.sum(total, axis=1, keepdims=True)
    line = jnp.sum(jnp.where(row8 == lane8, column, 0.0), axis=0, keepdims=True)
    out[0] = line[:, 0:K]

    for copy in sends:
        copy.wait_send()

    for n in range(count):
        for copy in [z_copy(n)] + y_copies(n) + relay_copies(n):
            copy.wait_send()
        for far in range(2):
            c_copy(n, far).wait_send()
    pair_c.wait_send()
    pair_r.wait_send()
    pair_t.wait_send()

    @pl.when(s < n_seg - 1)
    def _():
        for h in range(2):
            f_copy(h).wait_send()

    @pl.when(s > 0)
    def _():
        for m in range(2):
            for h in range(2):
                b_copy(m, h).wait_send()


def per_device(mesh_shape, centers, box_radii, labels, certified, conv_weights, conv_bias,
               head_weight, head_bias):
    n_seg, n_rep, n_box = (mesh_shape[a] for a in ("segment", "rep", "box"))
    h = conv_weights.shape[-1]
    classes = head_bias.shape[0]
    dma = pltpu.SemaphoreType.DMA
    vmem = pl.BlockSpec(memory_space=pltpu.VMEM)
    hbm = pl.BlockSpec(memory_space=pl.ANY)
    return pl.pallas_call(
        functools.partial(kernel, n_seg, n_rep, n_box, classes),
        out_shape=jax.ShapeDtypeStruct((1, 1, K), f32),
        in_specs=[hbm] * 8,
        out_specs=vmem,
        scratch_shapes=[
            pltpu.SMEM(certified.shape, jnp.int32),
            pltpu.SMEM(labels.shape, jnp.int32),
            pltpu.VMEM(conv_bias.shape, f32),
            pltpu.VMEM((classes, h), bf16),
            pltpu.VMEM((1, classes), f32),
            pltpu.VMEM((TAPS, h, h), bf16),
            pltpu.VMEM((TAPS, 80, 128), bf16),
            pltpu.VMEM((TAPS, 80, h), bf16),
            pltpu.VMEM((128, h), bf16),
            pltpu.VMEM((8, 4, 4, h), f32),
            pltpu.VMEM((8, 4, 4, h), f32),
            pltpu.VMEM((2, 8, 128), f32),
            pltpu.VMEM((64, h), f32),
            pltpu.VMEM((2, 64, h // 2), bf16),
            pltpu.VMEM((2, 64, h // 2), bf16),
            pltpu.VMEM((2, 2, 80, h // 2), bf16),
            pltpu.VMEM((2, 2, 80, h // 2), bf16),
            pltpu.VMEM((2, 80, h), f32),
            pltpu.VMEM((2, 80, h), f32),
            pltpu.VMEM((2, 64, h // 2), f32),
            pltpu.VMEM((2, 16, h), f32),
            pltpu.VMEM((2, 16, h), f32),
            pltpu.VMEM((2, 8, h), f32),
            pltpu.VMEM((16, 128), f32),
            pltpu.VMEM((2 * n_seg, 16, 128), f32),
            dma((8,)),
            dma((len(TREE),)),
            dma((len(TREE),)),
            dma((len(TREE), 4)),
            dma((len(TREE), 4)),
            dma((len(TREE), 2)),
            dma((len(TREE), 2)),
            dma((3,)),
            dma((3,)),
            dma((2,)),
            dma((2,)),
            dma((2, 2)),
            dma((2, 2)),
            dma((2 * n_seg,)),
            dma((2 * n_seg,)),
        ],
        compiler_params=pltpu.CompilerParams(collective_id=0, has_side_effects=True),
    )(certified, labels, centers, box_radii, conv_weights, conv_bias, head_weight.T,
      head_bias[None, :])


def solution(mesh):
    placed = (
        P(("rep", "box"), None, None, None),
        P(("rep", "box"), None, None, None),
        P(("rep", "box")),
        P(("rep", "box")),
        P("segment", None, "box", None),
        P("segment", None),
        P(),
        P(),
    )
    return jax.shard_map(
        functools.partial(per_device, dict(mesh.shape)),
        mesh=mesh,
        in_specs=placed,
        out_specs=P(("rep", "box"), "segment", None),
        check_vma=False,
    )
```

```python
import functools

import jax
import jax.numpy as jnp
from jax import lax
from jax.experimental import pallas as pl
from jax.experimental.pallas import tpu as pltpu
from jax.sharding import PartitionSpec as P

K = 5
TAPS = 9
TREE = ((2,0),(-2,0),(4,2),(-4,-2),(3,2),(-3,-2),(6,4),(-6,-4),(5,4),(-5,-4),(8,6),(7,6),(-7,-6),(1,0),(-1,0))
FIRST = (2,-2,1,-1)
WHOLE = (1, -1)
LAG = 5
LAG2 = 9
bf16 = jnp.bfloat16
f32 = jnp.float32
MESH = pl.DeviceIdType.MESH


def kernel(
    n_seg, n_rep, n_box, classes,
    cert_in, lab_in, cen, rad, cw, bias_in, hw_in, hb_in, out,
    cert, lab, bias, hw, hb, W, S, L, G, C8, R8, PT, MID, fin, fout, cin, cout, CF, NEW, ACC, slope, cept, HC, HO, T,
    loc, zs, zr, ys, yr, cs, cr, xs, xr, fs, fr, bs, br, ts, tr,
):
    s = lax.axis_index("segment")
    r = lax.axis_index("rep")
    z = lax.axis_index("box")
    c = lax.rem(r, 2)
    mate = {"rep": r + 1 - 2 * c}
    y_up = {"rep": lax.rem(r + 2, n_rep)}
    y_down = {"rep": lax.rem(r + n_rep - 2, n_rep)}
    jumps = sorted({o - p for o, p in TREE} | {p - o for o, p in TREE})

    def along(o):
        return {"box": lax.rem(z + n_box + o, n_box)}

    peers = []
    for dx in range(n_seg):
        for dc in range(2):
            if dx or dc:
                peers.append(
                    {"segment": lax.rem(s + dx, n_seg), "rep": r + dc * (1 - 2 * c)}
                )
    shard = W.shape[1] // n_box
    half = shard // 2
    rows_y = n_rep // 2
    y = r // 2
    wide = W.shape[2] // 2
    slim = W.shape[2] // rows_y
    mid_tap = TAPS // 2

    own = pltpu.make_async_copy(
        cw.at[0], W.at[:, pl.ds(pl.multiple_of(z * shard, shard), shard), :], loc.at[0]
    )
    own.start()
    own_c = pltpu.make_async_copy(cen, C8.at[pl.ds(4 * c, 4)], loc.at[1])
    own_c.start()
    own_r = pltpu.make_async_copy(rad, R8.at[pl.ds(4 * c, 4)], loc.at[2])
    own_r.start()
    small = []
    for n, (there, here) in enumerate(
        ((cert_in, cert), (lab_in, lab), (bias_in, bias), (hw_in, hw), (hb_in, hb))
    ):
        copy = pltpu.make_async_copy(there, here, loc.at[3 + n])
        copy.start()
        small.append(copy)

    barrier = pltpu.get_barrier_semaphore()
    near = [y_up, y_down] + [along(o) for o in jumps] + peers
    for device in near:
        pl.semaphore_signal(barrier, inc=1, device_id=device, device_id_type=MESH)
    pl.semaphore_wait(barrier, len(near))

    def remote(src, dst, send, recv, device):
        return pltpu.make_async_remote_copy(
            src_ref=src, dst_ref=dst, send_sem=send, recv_sem=recv,
            device_id=device, device_id_type=MESH,
        )

    def piece(n, core, taps, lane, width, back=0):
        b = lax.rem(z + 2 * n_box - TREE[n][0] + back, n_box)
        row = pl.multiple_of(b * shard + core * half, half)
        lane = pl.multiple_of(lane, width) if width < 2 * wide else 0
        return W.at[pl.ds(taps[0], taps[1] - taps[0]), pl.ds(row, half), pl.ds(lane, width)]

    every, low_part, high_part = (0, TAPS), (0, mid_tap), (mid_tap, TAPS)
    y_next, y_prev = lax.rem(y + 1, rows_y), lax.rem(y + rows_y - 1, rows_y)
    y_far = lax.rem(y + 2, rows_y)

    def z_copy(n, arriving=False):
        offset, parent = TREE[n]
        back = 0 if arriving else offset - parent
        lane, width = (0, 2 * wide) if offset in WHOLE else (y * slim, slim)
        ref = piece(n, c, every, lane, width, back)
        return remote(ref, ref, zs.at[n], zr.at[n], along(offset - parent))

    def y_copies(n, arriving=False):
        out = []
        for d in () if TREE[n][0] in WHOLE else range(2):
            part = (y_prev, y_next)[d] if arriving else y
            ref = piece(n, c, every, part * slim, slim)
            out.append(remote(ref, ref, ys.at[n, d], yr.at[n, d], (y_up, y_down)[d]))
        return out

    def relay_copies(n, arriving=False):
        out = []
        for d in () if TREE[n][0] in WHOLE else range(2):
            part = y_far if arriving else (y_prev, y_next)[d]
            ref = piece(n, c, (low_part, high_part)[d], part * slim, slim)
            out.append(remote(ref, ref, ys.at[n, 2 + d], yr.at[n, 2 + d], (y_up, y_down)[d]))
        return out

    near_half = y // 2

    def c_copy(n, far, arriving=False):
        side = 1 - near_half if far else near_half
        ref = piece(n, 1 - c if arriving else c, every, side * wide, wide)
        return remote(ref, ref, cs.at[n, far], cr.at[n, far], mate)

    own.wait()
    index = {offset: n for n, (offset, _) in enumerate(TREE)}
    for offset in FIRST:
        z_copy(index[offset]).start()

    own_c.wait()
    own_r.wait()
    for copy in small:
        copy.wait()
    pair_c = remote(C8.at[pl.ds(4 * c, 4)], C8.at[pl.ds(4 * c, 4)], xs.at[0], xr.at[0], mate)
    pair_r = remote(R8.at[pl.ds(4 * c, 4)], R8.at[pl.ds(4 * c, 4)], xs.at[1], xr.at[1], mate)
    row8 = lax.broadcasted_iota(jnp.int32, (8, 128), 0)
    lane8 = lax.broadcasted_iota(jnp.int32, (8, 128), 1)
    tile = jnp.zeros((8, 128), f32)
    for i in range(4):
        alive_i = (1 - cert[i]).astype(f32)
        label_i = lab[i].astype(f32)
        here = lane8 == 4 * c + i
        tile = jnp.where(here & (row8 == 0), alive_i, tile)
        tile = jnp.where(here & (row8 == 1), label_i, tile)
    PT[c] = tile
    pair_t = remote(PT.at[c], PT.at[c], xs.at[2], xr.at[2], mate)
    pair_t.start()
    pair_c.start()
    pair_r.start()

    p_row = lax.broadcasted_iota(jnp.int32, (80, 128), 0)
    p_col = lax.broadcasted_iota(jnp.int32, (80, 128), 1)
    same = (p_row // 16) == (p_col // 16)
    dy = lax.rem(p_col, 16) // 4 - lax.rem(p_row, 16) // 4
    dx_ = lax.rem(p_col, 4) - lax.rem(p_row, 4)
    for t in range(TAPS):
        a, b = divmod(t, 3)
        S[t] = jnp.where(same & (dy == a - 1) & (dx_ == b - 1), 1.0, 0.0).astype(bf16)
    G[...] = jnp.zeros_like(G)

    count = len(TREE)

    def take_relayed(n):
        for copy in relay_copies(n, True):
            copy.wait_recv()
        if TREE[n][0] not in WHOLE:
            c_copy(n, 1).start()

    for n in range(count + LAG):
        if n < count:
            z_copy(n, True).wait_recv()
            for child, (_, parent) in enumerate(TREE):
                if parent == TREE[n][0]:
                    z_copy(child).start()
            for copy in y_copies(n):
                copy.start()
            if TREE[n][0] in WHOLE:
                for far in range(2):
                    c_copy(n, far).start()
        if n >= LAG:
            for copy in y_copies(n - LAG, True):
                copy.wait_recv()
            for copy in relay_copies(n - LAG):
                copy.start()
            if TREE[n - LAG][0] not in WHOLE:
                c_copy(n - LAG, 0).start()
        if n >= LAG2:
            take_relayed(n - LAG2)

    remote(PT.at[1 - c], PT.at[1 - c], xs.at[2], xr.at[2], mate).wait_recv()
    other = pl.ds(4 * (1 - c), 4)
    remote(C8.at[other], C8.at[other], xs.at[0], xr.at[0], mate).wait_recv()
    remote(R8.at[other], R8.at[other], xs.at[1], xr.at[1], mate).wait_recv()
    both = PT[0] + PT[1]
    alive_row = both[0:1, :]
    label_row = both[1:2, :]
    alive = jnp.sum(jnp.where(lane8 == row8, alive_row, 0.0), axis=1, keepdims=True)
    labels = jnp.sum(jnp.where(lane8 == row8, label_row, 0.0), axis=1, keepdims=True)
    rank = jnp.sum(jnp.where(lane8 < row8, alive_row, 0.0), axis=1, keepdims=True)
    live_no = jnp.where(alive > 0.5, rank, -1.0)
    first = (2 * c).astype(f32)

    @pl.when(s == 0)
    def _():
        for m in range(2):
            pick = jnp.where(live_no == first + m, 1.0, 0.0)
            middle = jnp.zeros((16, C8.shape[3]), f32)
            radius = jnp.zeros((16, C8.shape[3]), f32)
            for i in range(8):
                take = pick[i : i + 1, :] > 0.5
                middle = jnp.where(take, C8[i].reshape(middle.shape), middle)
                radius = jnp.where(take, R8[i].reshape(radius.shape), radius)
            MID[16 * m : 16 * m + 16] = middle
            MID[32 + 16 * m : 48 + 16 * m] = radius

    @pl.when(s == n_seg - 1)
    def _():
        row = lax.broadcasted_iota(jnp.int32, (16, 1), 0)
        spec = lax.rem(row, 8).astype(f32)
        lab0 = jnp.sum(jnp.where(live_no == first, labels, 0.0), axis=0, keepdims=True)
        lab1 = jnp.sum(jnp.where(live_no == first + 1.0, labels, 0.0), axis=0, keepdims=True)
        true = jnp.where(row < 8, lab0, lab1)
        rival = true + 1.0 + spec
        rival = jnp.where(rival >= classes, rival - classes, rival)
        ids = lax.broadcasted_iota(jnp.int32, (16, classes), 1).astype(f32)
        selector = jnp.where(ids == true, 1.0, 0.0) - jnp.where(ids == rival, 1.0, 0.0)
        selector = jnp.where(spec < K, selector, 0.0)
        pooled = lax.dot_general(
            selector.astype(bf16), hw[...], (((1,), (0,)), ((), ())), preferred_element_type=f32
        ) / 16.0
        HC[...] = pooled.reshape(2, 8, pooled.shape[1])
        offset = jnp.sum(selector * hb[...], axis=1, keepdims=True)
        lane16 = lax.broadcasted_iota(jnp.int32, (16, 128), 1)
        HO[...] = jnp.where(lane16 == 0, offset, 0.0)

    up_x = {"segment": lax.rem(s + 1, n_seg)}
    down_x = {"segment": lax.rem(s + n_seg - 1, n_seg)}
    part_h = W.shape[1] // 2
    cols = [slice(h * part_h, (h + 1) * part_h) for h in range(2)]
    rows_in = (((1,), (1,)), ((), ()))

    def f_copy(h):
        return remote(fout.at[h], fin.at[h], fs.at[h], fr.at[h], up_x)

    def b_copy(m, h):
        return remote(cout.at[m, h], cin.at[m, h], bs.at[m, h], br.at[m, h], down_x)

    def half_forward(h, finish):
        here = pl.ds(pl.multiple_of(h * part_h, part_h), part_h)
        G[0:64, here] = MID[:, here].astype(bf16)
        for t in range(TAPS):
            L[t, 0:64, here] = jnp.dot(
                S[t, 0:64], G[:, here], preferred_element_type=f32
            ).astype(bf16)
        for n in range(2):
            start = ACC[n] if finish else jnp.zeros((64, part_h), f32)
            centre, spread = start[0:32], start[32:64]
            for t in range(TAPS):
                w = W[t, cols[n], here]
                centre += lax.dot_general(
                    L[t, 0:32, here], w, rows_in, preferred_element_type=f32
                )
                spread += lax.dot_general(
                    L[t, 32:64, here], jnp.abs(w), rows_in, preferred_element_type=f32
                )
            if not finish:
                ACC[n, 0:32] = centre
                ACC[n, 32:64] = spread
                continue
            centre = centre + bias[:, cols[n]]
            low = centre - spread
            up = centre + spread
            up_pos = jnp.maximum(up, 0.0)
            low_pos = jnp.maximum(low, 0.0)
            low_neg = jnp.maximum(-low, 0.0)
            fout[n, 0:32] = (MID[0:32, cols[n]] + 0.5 * (up_pos + low_pos)).astype(bf16)
            fout[n, 32:64] = (MID[32:64, cols[n]] + 0.5 * (up_pos - low_pos)).astype(bf16)

            @pl.when(s < n_seg - 1)
            def _():
                f_copy(n).start()

            slope_now = up_pos / (up_pos + low_neg)
            cept_now = slope_now * low_neg
            for m in range(2):
                slope[m, :, cols[n]] = slope_now[16 * m : 16 * m + 16]
                cept[m, :, cols[n]] = cept_now[16 * m : 16 * m + 16]

    for n in range(count):
        c_copy(n, 0, True).wait_recv()

    @pl.when(s == 0)
    def _():
        half_forward(near_half, False)

    for n in range(count + LAG - LAG2, count):
        take_relayed(n)
    for n in range(count):
        c_copy(n, 1, True).wait_recv()

    @pl.when(s > 0)
    def _():
        f_copy(0).wait_recv()
        MID[:, cols[0]] = fin[0].astype(f32)
        half_forward(0, False)
        f_copy(1).wait_recv()
        MID[:, cols[1]] = fin[1].astype(f32)

    half_forward(jnp.where(s == 0, 1 - near_half, 1), True)

    slot = s * 2 + c

    def terms(m):
        for k in range(K):
            rows = slice(16 * k, 16 * k + 16)
            now = CF[m, rows]
            part = now * slope[m] * bias[...] + jnp.minimum(now, 0.0) * cept[m]
            new_k = NEW[m, rows]
            ends = new_k * MID[16 * m : 16 * m + 16] - jnp.abs(new_k) * MID[
                32 + 16 * m : 48 + 16 * m
            ]
            part = part + jnp.where(s == 0, ends, 0.0)
            part = jnp.sum(part, axis=0, keepdims=True)
            folded = part[:, 0:128]
            for q in range(1, part.shape[1] // 128):
                folded = folded + part[:, 128 * q : 128 * q + 128]
            at = 8 * m + k
            folded = folded + jnp.where(s == n_seg - 1, HO[at : at + 1, :], 0.0)
            T[slot, at : at + 1, :] = folded

    for m in range(2):
        for h in range(2):
            @pl.when(s == n_seg - 1)
            def _():
                for k in range(K):
                    CF[m, 16 * k : 16 * k + 16, cols[h]] = jnp.broadcast_to(
                        HC[m, k : k + 1, cols[h]], (16, part_h)
                    )

            @pl.when(s < n_seg - 1)
            def _():
                b_copy(m, h).wait_recv()
                CF[m, :, cols[h]] = cin[m, h].astype(f32)

            slope_m = slope[m, :, cols[h]]
            for k in range(K):
                rows = slice(16 * k, 16 * k + 16)
                G[rows, cols[h]] = (CF[m, rows, cols[h]] * slope_m).astype(bf16)
            for t in range(TAPS):
                L[t, :, cols[h]] = jnp.dot(
                    S[TAPS - 1 - t], G[:, cols[h]], preferred_element_type=f32
                ).astype(bf16)
            for n in range(2):
                new = NEW[m, :, cols[n]] if h else jnp.zeros((80, part_h), f32)
                for t in range(TAPS):
                    new += jnp.dot(
                        L[t, :, cols[h]], W[t, cols[h], cols[n]], preferred_element_type=f32
                    )
                if h == 0:
                    NEW[m, :, cols[n]] = new
                    continue
                new = new + CF[m, :, cols[n]]
                NEW[m, :, cols[n]] = new

                @pl.when(s > 0)
                def _():
                    cout[m, n] = new.astype(bf16)
                    b_copy(m, n).start()

        if m == 0:
            pl.when(s == 0)(functools.partial(terms, 0))

    pl.when(s > 0)(functools.partial(terms, 0))
    terms(1)

    sends = []
    for n, device in enumerate(peers):
        copy = remote(T.at[slot], T.at[slot], ts.at[n], tr.at[slot], device)
        copy.start()
        sends.append(copy)
    for dx in range(n_seg):
        for dc in range(2):
            if dx or dc:
                there = lax.rem(s + dx, n_seg) * 2 + c + dc * (1 - 2 * c)
                remote(T.at[there], T.at[there], ts.at[0], tr.at[there], mate).wait_recv()
    mine = jnp.where(row8[:, 0:1] == 4 * c + s, live_no, -1.0)
    mine = jnp.max(mine, axis=0, keepdims=True)
    total = jnp.zeros((8, 128), f32)
    for core in range(2):
        for m in range(2):
            part = T[core, 8 * m : 8 * m + 8]
            for x in range(1, n_seg):
                part = part + T[2 * x + core, 8 * m : 8 * m + 8]
            total = jnp.where((mine == float(2 * core + m)) & (row8 < K), part, total)
    column = jnp.sum(total, axis=1, keepdims=True)
    line = jnp.sum(jnp.where(row8 == lane8, column, 0.0), axis=0, keepdims=True)
    out[0] = line[:, 0:K]

    for copy in sends:
        copy.wait_send()

    for n in range(count):
        for copy in [z_copy(n)] + y_copies(n) + relay_copies(n):
            copy.wait_send()
        for far in range(2):
            c_copy(n, far).wait_send()
    pair_c.wait_send()
    pair_r.wait_send()
    pair_t.wait_send()

    @pl.when(s < n_seg - 1)
    def _():
        for h in range(2):
            f_copy(h).wait_send()

    @pl.when(s > 0)
    def _():
        for m in range(2):
            for h in range(2):
                b_copy(m, h).wait_send()


def per_device(mesh_shape, centers, box_radii, labels, certified, conv_weights, conv_bias,
               head_weight, head_bias):
    n_seg, n_rep, n_box = (mesh_shape[a] for a in ("segment", "rep", "box"))
    h = conv_weights.shape[-1]
    classes = head_bias.shape[0]
    dma = pltpu.SemaphoreType.DMA
    vmem = pl.BlockSpec(memory_space=pltpu.VMEM)
    hbm = pl.BlockSpec(memory_space=pl.ANY)
    return pl.pallas_call(
        functools.partial(kernel, n_seg, n_rep, n_box, classes),
        out_shape=jax.ShapeDtypeStruct((1, 1, K), f32),
        in_specs=[hbm] * 8,
        out_specs=vmem,
        scratch_shapes=[
            pltpu.SMEM(certified.shape, jnp.int32),
            pltpu.SMEM(labels.shape, jnp.int32),
            pltpu.VMEM(conv_bias.shape, f32),
            pltpu.VMEM((classes, h), bf16),
            pltpu.VMEM((1, classes), f32),
            pltpu.VMEM((TAPS, h, h), bf16),
            pltpu.VMEM((TAPS, 80, 128), bf16),
            pltpu.VMEM((TAPS, 80, h), bf16),
            pltpu.VMEM((128, h), bf16),
            pltpu.VMEM((8, 4, 4, h), f32),
            pltpu.VMEM((8, 4, 4, h), f32),
            pltpu.VMEM((2, 8, 128), f32),
            pltpu.VMEM((64, h), f32),
            pltpu.VMEM((2, 64, h // 2), bf16),
            pltpu.VMEM((2, 64, h // 2), bf16),
            pltpu.VMEM((2, 2, 80, h // 2), bf16),
            pltpu.VMEM((2, 2, 80, h // 2), bf16),
            pltpu.VMEM((2, 80, h), f32),
            pltpu.VMEM((2, 80, h), f32),
            pltpu.VMEM((2, 64, h // 2), f32),
            pltpu.VMEM((2, 16, h), f32),
            pltpu.VMEM((2, 16, h), f32),
            pltpu.VMEM((2, 8, h), f32),
            pltpu.VMEM((16, 128), f32),
            pltpu.VMEM((2 * n_seg, 16, 128), f32),
            dma((8,)),
            dma((len(TREE),)),
            dma((len(TREE),)),
            dma((len(TREE), 4)),
            dma((len(TREE), 4)),
            dma((len(TREE), 2)),
            dma((len(TREE), 2)),
            dma((3,)),
            dma((3,)),
            dma((2,)),
            dma((2,)),
            dma((2, 2)),
            dma((2, 2)),
            dma((2 * n_seg,)),
            dma((2 * n_seg,)),
        ],
        compiler_params=pltpu.CompilerParams(collective_id=0, has_side_effects=True),
    )(certified, labels, centers, box_radii, conv_weights, conv_bias, head_weight.T,
      head_bias[None, :])


def solution(mesh):
    placed = (
        P(("rep", "box"), None, None, None),
        P(("rep", "box"), None, None, None),
        P(("rep", "box")),
        P(("rep", "box")),
        P("segment", None, "box", None),
        P("segment", None),
        P(),
        P(),
    )
    return jax.shard_map(
        functools.partial(per_device, dict(mesh.shape)),
        mesh=mesh,
        in_specs=placed,
        out_specs=P(("rep", "box"), "segment", None),
        check_vma=False,
    )
```

```python
import functools

import jax
import jax.numpy as jnp
from jax import lax
from jax.experimental import pallas as pl
from jax.experimental.pallas import tpu as pltpu
from jax.sharding import PartitionSpec as P

K = 5
TAPS = 9
TREE = ((2,0),(-2,0),(4,2),(-4,-2),(3,2),(-3,-2),(6,4),(-6,-4),(5,4),(-5,-4),(8,6),(7,6),(-7,-6),(1,0),(-1,0))
FIRST = (2,-2,1,-1)
WHOLE = (1, -1)
LAG = 5
LAG2 = 9
bf16 = jnp.bfloat16
f32 = jnp.float32
MESH = pl.DeviceIdType.MESH


def kernel(
    n_seg, n_rep, n_box, classes,
    cert_in, lab_in, cen, rad, cw, bias_in, hw_in, hb_in, out,
    cert, lab, bias, hw, hb, W, S, L, G, C8, R8, PT, MID, fin, fout, cin, cout, CF, NEW, ACC, slope, cept, HC, HO, T,
    loc, zs, zr, ys, yr, cs, cr, xs, xr, fs, fr, bs, br, ts, tr,
):
    s = lax.axis_index("segment")
    r = lax.axis_index("rep")
    z = lax.axis_index("box")
    c = lax.rem(r, 2)
    mate = {"rep": r + 1 - 2 * c}
    y_up = {"rep": lax.rem(r + 2, n_rep)}
    y_down = {"rep": lax.rem(r + n_rep - 2, n_rep)}
    jumps = sorted({o - p for o, p in TREE} | {p - o for o, p in TREE})

    def along(o):
        return {"box": lax.rem(z + n_box + o, n_box)}

    peers = []
    for dx in range(n_seg):
        for dc in range(2):
            if dx or dc:
                peers.append(
                    {"segment": lax.rem(s + dx, n_seg), "rep": r + dc * (1 - 2 * c)}
                )
    shard = W.shape[1] // n_box
    half = shard // 2
    rows_y = n_rep // 2
    y = r // 2
    wide = W.shape[2] // 2
    slim = W.shape[2] // rows_y
    mid_tap = TAPS // 2

    own = pltpu.make_async_copy(
        cw.at[0], W.at[:, pl.ds(pl.multiple_of(z * shard, shard), shard), :], loc.at[0]
    )
    own.start()
    own_c = pltpu.make_async_copy(cen, C8.at[pl.ds(4 * c, 4)], loc.at[1])
    own_c.start()
    own_r = pltpu.make_async_copy(rad, R8.at[pl.ds(4 * c, 4)], loc.at[2])
    own_r.start()
    small = []
    for n, (there, here) in enumerate(
        ((cert_in, cert), (lab_in, lab), (bias_in, bias), (hw_in, hw), (hb_in, hb))
    ):
        copy = pltpu.make_async_copy(there, here, loc.at[3 + n])
        copy.start()
        small.append(copy)

    barrier = pltpu.get_barrier_semaphore()
    near = [y_up, y_down] + [along(o) for o in jumps] + peers
    for device in near:
        pl.semaphore_signal(barrier, inc=1, device_id=device, device_id_type=MESH)
    pl.semaphore_wait(barrier, len(near))

    def remote(src, dst, send, recv, device):
        return pltpu.make_async_remote_copy(
            src_ref=src, dst_ref=dst, send_sem=send, recv_sem=recv,
            device_id=device, device_id_type=MESH,
        )

    def piece(n, core, taps, lane, width, back=0):
        b = lax.rem(z + 2 * n_box - TREE[n][0] + back, n_box)
        row = pl.multiple_of(b * shard + core * half, half)
        lane = pl.multiple_of(lane, width) if width < 2 * wide else 0
        return W.at[pl.ds(taps[0], taps[1] - taps[0]), pl.ds(row, half), pl.ds(lane, width)]

    every, low_part, high_part = (0, TAPS), (0, mid_tap), (mid_tap, TAPS)
    y_next, y_prev = lax.rem(y + 1, rows_y), lax.rem(y + rows_y - 1, rows_y)
    y_far = lax.rem(y + 2, rows_y)

    def z_copy(n, arriving=False):
        offset, parent = TREE[n]
        back = 0 if arriving else offset - parent
        lane, width = (0, 2 * wide) if offset in WHOLE else (y * slim, slim)
        ref = piece(n, c, every, lane, width, back)
        return remote(ref, ref, zs.at[n], zr.at[n], along(offset - parent))

    def y_copies(n, arriving=False):
        out = []
        for d in () if TREE[n][0] in WHOLE else range(2):
            part = (y_prev, y_next)[d] if arriving else y
            ref = piece(n, c, every, part * slim, slim)
            out.append(remote(ref, ref, ys.at[n, d], yr.at[n, d], (y_up, y_down)[d]))
        return out

    def relay_copies(n, arriving=False):
        out = []
        for d in () if TREE[n][0] in WHOLE else range(2):
            part = y_far if arriving else (y_prev, y_next)[d]
            ref = piece(n, c, (low_part, high_part)[d], part * slim, slim)
            out.append(remote(ref, ref, ys.at[n, 2 + d], yr.at[n, 2 + d], (y_up, y_down)[d]))
        return out

    near_half = y // 2

    def c_copy(n, far, arriving=False):
        side = 1 - near_half if far else near_half
        ref = piece(n, 1 - c if arriving else c, every, side * wide, wide)
        return remote(ref, ref, cs.at[n, far], cr.at[n, far], mate)

    own.wait()
    index = {offset: n for n, (offset, _) in enumerate(TREE)}
    for offset in FIRST:
        z_copy(index[offset]).start()

    own_c.wait()
    own_r.wait()
    for copy in small:
        copy.wait()
    pair_c = remote(C8.at[pl.ds(4 * c, 4)], C8.at[pl.ds(4 * c, 4)], xs.at[0], xr.at[0], mate)
    pair_r = remote(R8.at[pl.ds(4 * c, 4)], R8.at[pl.ds(4 * c, 4)], xs.at[1], xr.at[1], mate)
    row8 = lax.broadcasted_iota(jnp.int32, (8, 128), 0)
    lane8 = lax.broadcasted_iota(jnp.int32, (8, 128), 1)
    tile = jnp.zeros((8, 128), f32)
    for i in range(4):
        alive_i = (1 - cert[i]).astype(f32)
        label_i = lab[i].astype(f32)
        here = lane8 == 4 * c + i
        tile = jnp.where(here & (row8 == 0), alive_i, tile)
        tile = jnp.where(here & (row8 == 1), label_i, tile)
    PT[c] = tile
    pair_t = remote(PT.at[c], PT.at[c], xs.at[2], xr.at[2], mate)
    pair_t.start()
    pair_c.start()
    pair_r.start()

    p_row = lax.broadcasted_iota(jnp.int32, (80, 128), 0)
    p_col = lax.broadcasted_iota(jnp.int32, (80, 128), 1)
    same = (p_row // 16) == (p_col // 16)
    dy = lax.rem(p_col, 16) // 4 - lax.rem(p_row, 16) // 4
    dx_ = lax.rem(p_col, 4) - lax.rem(p_row, 4)
    for t in range(TAPS):
        a, b = divmod(t, 3)
        S[t] = jnp.where(same & (dy == a - 1) & (dx_ == b - 1), 1.0, 0.0).astype(bf16)
    G[...] = jnp.zeros_like(G)

    count = len(TREE)

    def take_relayed(n):
        for copy in relay_copies(n, True):
            copy.wait_recv()
        if TREE[n][0] not in WHOLE:
            c_copy(n, 1).start()

    for n in range(count + LAG):
        if n < count:
            z_copy(n, True).wait_recv()
            for child, (_, parent) in enumerate(TREE):
                if parent == TREE[n][0]:
                    z_copy(child).start()
            for copy in y_copies(n):
                copy.start()
            if TREE[n][0] in WHOLE:
                for far in range(2):
                    c_copy(n, far).start()
        if n >= LAG:
            for copy in y_copies(n - LAG, True):
                copy.wait_recv()
            for copy in relay_copies(n - LAG):
                copy.start()
            if TREE[n - LAG][0] not in WHOLE:
                c_copy(n - LAG, 0).start()
        if n >= LAG2:
            take_relayed(n - LAG2)

    remote(PT.at[1 - c], PT.at[1 - c], xs.at[2], xr.at[2], mate).wait_recv()
    other = pl.ds(4 * (1 - c), 4)
    remote(C8.at[other], C8.at[other], xs.at[0], xr.at[0], mate).wait_recv()
    remote(R8.at[other], R8.at[other], xs.at[1], xr.at[1], mate).wait_recv()
    both = PT[0] + PT[1]
    alive_row = both[0:1, :]
    label_row = both[1:2, :]
    alive = jnp.sum(jnp.where(lane8 == row8, alive_row, 0.0), axis=1, keepdims=True)
    labels = jnp.sum(jnp.where(lane8 == row8, label_row, 0.0), axis=1, keepdims=True)
    rank = jnp.sum(jnp.where(lane8 < row8, alive_row, 0.0), axis=1, keepdims=True)
    live_no = jnp.where(alive > 0.5, rank, -1.0)
    first = (2 * c).astype(f32)

    @pl.when(s == 0)
    def _():
        for m in range(2):
            pick = jnp.where(live_no == first + m, 1.0, 0.0)
            middle = jnp.zeros((16, C8.shape[3]), f32)
            radius = jnp.zeros((16, C8.shape[3]), f32)
            for i in range(8):
                take = pick[i : i + 1, :] > 0.5
                middle = jnp.where(take, C8[i].reshape(middle.shape), middle)
                radius = jnp.where(take, R8[i].reshape(radius.shape), radius)
            MID[16 * m : 16 * m + 16] = middle
            MID[32 + 16 * m : 48 + 16 * m] = radius

    @pl.when(s == n_seg - 1)
    def _():
        row = lax.broadcasted_iota(jnp.int32, (16, 1), 0)
        spec = lax.rem(row, 8).astype(f32)
        lab0 = jnp.sum(jnp.where(live_no == first, labels, 0.0), axis=0, keepdims=True)
        lab1 = jnp.sum(jnp.where(live_no == first + 1.0, labels, 0.0), axis=0, keepdims=True)
        true = jnp.where(row < 8, lab0, lab1)
        rival = true + 1.0 + spec
        rival = jnp.where(rival >= classes, rival - classes, rival)
        ids = lax.broadcasted_iota(jnp.int32, (16, classes), 1).astype(f32)
        selector = jnp.where(ids == true, 1.0, 0.0) - jnp.where(ids == rival, 1.0, 0.0)
        selector = jnp.where(spec < K, selector, 0.0)
        pooled = lax.dot_general(
            selector.astype(bf16), hw[...], (((1,), (0,)), ((), ())), preferred_element_type=f32
        ) / 16.0
        HC[...] = pooled.reshape(2, 8, pooled.shape[1])
        offset = jnp.sum(selector * hb[...], axis=1, keepdims=True)
        lane16 = lax.broadcasted_iota(jnp.int32, (16, 128), 1)
        HO[...] = jnp.where(lane16 == 0, offset, 0.0)

    up_x = {"segment": lax.rem(s + 1, n_seg)}
    down_x = {"segment": lax.rem(s + n_seg - 1, n_seg)}
    part_h = W.shape[1] // 2
    cols = [slice(h * part_h, (h + 1) * part_h) for h in range(2)]
    rows_in = (((1,), (1,)), ((), ()))

    def f_copy(h):
        return remote(fout.at[h], fin.at[h], fs.at[h], fr.at[h], up_x)

    def b_copy(m, h):
        return remote(cout.at[m, h], cin.at[m, h], bs.at[m, h], br.at[m, h], down_x)

    def half_forward(h, finish):
        here = pl.ds(pl.multiple_of(h * part_h, part_h), part_h)
        G[0:64, here] = MID[:, here].astype(bf16)
        for t in range(TAPS):
            L[t, 0:64, here] = jnp.dot(
                S[t, 0:64], G[:, here], preferred_element_type=f32
            ).astype(bf16)
        for n in range(2):
            start = ACC[n] if finish else jnp.zeros((64, part_h), f32)
            centre, spread = start[0:32], start[32:64]
            for t in range(TAPS):
                w = W[t, cols[n], here]
                centre += lax.dot_general(
                    L[t, 0:32, here], w, rows_in, preferred_element_type=f32
                )
                spread += lax.dot_general(
                    L[t, 32:64, here], jnp.abs(w), rows_in, preferred_element_type=f32
                )
            if not finish:
                ACC[n, 0:32] = centre
                ACC[n, 32:64] = spread
                continue
            centre = centre + bias[:, cols[n]]
            low = centre - spread
            up = centre + spread
            up_pos = jnp.maximum(up, 0.0)
            low_pos = jnp.maximum(low, 0.0)
            low_neg = jnp.maximum(-low, 0.0)
            fout[n, 0:32] = (MID[0:32, cols[n]] + 0.5 * (up_pos + low_pos)).astype(bf16)
            fout[n, 32:64] = (MID[32:64, cols[n]] + 0.5 * (up_pos - low_pos)).astype(bf16)

            @pl.when(s < n_seg - 1)
            def _():
                f_copy(n).start()

            slope_now = up_pos / (up_pos + low_neg)
            cept_now = slope_now * low_neg
            for m in range(2):
                slope[m, :, cols[n]] = slope_now[16 * m : 16 * m + 16]
                cept[m, :, cols[n]] = cept_now[16 * m : 16 * m + 16]

    for n in range(count):
        c_copy(n, 0, True).wait_recv()

    @pl.when(s == 0)
    def _():
        half_forward(near_half, False)

    for n in range(count + LAG - LAG2, count):
        take_relayed(n)
    for n in range(count):
        c_copy(n, 1, True).wait_recv()

    @pl.when(s > 0)
    def _():
        f_copy(0).wait_recv()
        MID[:, cols[0]] = fin[0].astype(f32)
        half_forward(0, False)
        f_copy(1).wait_recv()
        MID[:, cols[1]] = fin[1].astype(f32)

    half_forward(jnp.where(s == 0, 1 - near_half, 1), True)

    slot = s * 2 + c

    def terms(m):
        for k in range(K):
            rows = slice(16 * k, 16 * k + 16)
            now = CF[m, rows]
            part = now * slope[m] * bias[...] + jnp.minimum(now, 0.0) * cept[m]
            new_k = NEW[m, rows]
            ends = new_k * MID[16 * m : 16 * m + 16] - jnp.abs(new_k) * MID[
                32 + 16 * m : 48 + 16 * m
            ]
            part = part + jnp.where(s == 0, ends, 0.0)
            part = jnp.sum(part, axis=0, keepdims=True)
            folded = part[:, 0:128]
            for q in range(1, part.shape[1] // 128):
                folded = folded + part[:, 128 * q : 128 * q + 128]
            at = 8 * m + k
            folded = folded + jnp.where(s == n_seg - 1, HO[at : at + 1, :], 0.0)
            T[slot, at : at + 1, :] = folded

    for m in range(2):
        for h in range(2):
            @pl.when(s == n_seg - 1)
            def _():
                for k in range(K):
                    CF[m, 16 * k : 16 * k + 16, cols[h]] = jnp.broadcast_to(
                        HC[m, k : k + 1, cols[h]], (16, part_h)
                    )

            @pl.when(s < n_seg - 1)
            def _():
                b_copy(m, h).wait_recv()
                CF[m, :, cols[h]] = cin[m, h].astype(f32)

            slope_m = slope[m, :, cols[h]]
            for k in range(K):
                rows = slice(16 * k, 16 * k + 16)
                G[rows, cols[h]] = (CF[m, rows, cols[h]] * slope_m).astype(bf16)
            for t in range(TAPS):
                L[t, :, cols[h]] = jnp.dot(
                    S[TAPS - 1 - t], G[:, cols[h]], preferred_element_type=f32
                ).astype(bf16)
            for n in range(2):
                new = NEW[m, :, cols[n]] if h else jnp.zeros((80, part_h), f32)
                for t in range(TAPS):
                    new += jnp.dot(
                        L[t, :, cols[h]], W[t, cols[h], cols[n]], preferred_element_type=f32
                    )
                if h == 0:
                    NEW[m, :, cols[n]] = new
                    continue
                new = new + CF[m, :, cols[n]]
                NEW[m, :, cols[n]] = new

                @pl.when(s > 0)
                def _():
                    cout[m, n] = new.astype(bf16)
                    b_copy(m, n).start()

        if m == 0:
            pl.when(s == 0)(functools.partial(terms, 0))

    pl.when(s > 0)(functools.partial(terms, 0))
    terms(1)

    sends = []
    for n, device in enumerate(peers):
        copy = remote(T.at[slot], T.at[slot], ts.at[n], tr.at[slot], device)
        copy.start()
        sends.append(copy)
    for n in range(count):
        for copy in [z_copy(n)] + y_copies(n) + relay_copies(n):
            copy.wait_send()
        for far in range(2):
            c_copy(n, far).wait_send()
    pair_c.wait_send()
    pair_r.wait_send()
    pair_t.wait_send()

    @pl.when(s < n_seg - 1)
    def _():
        for h in range(2):
            f_copy(h).wait_send()

    @pl.when(s > 0)
    def _():
        for m in range(2):
            for h in range(2):
                b_copy(m, h).wait_send()

    for dx in range(n_seg):
        for dc in range(2):
            if dx or dc:
                there = lax.rem(s + dx, n_seg) * 2 + c + dc * (1 - 2 * c)
                remote(T.at[there], T.at[there], ts.at[0], tr.at[there], mate).wait_recv()
    mine = jnp.where(row8[:, 0:1] == 4 * c + s, live_no, -1.0)
    mine = jnp.max(mine, axis=0, keepdims=True)
    total = jnp.zeros((8, 128), f32)
    for core in range(2):
        for m in range(2):
            part = T[core, 8 * m : 8 * m + 8]
            for x in range(1, n_seg):
                part = part + T[2 * x + core, 8 * m : 8 * m + 8]
            total = jnp.where((mine == float(2 * core + m)) & (row8 < K), part, total)
    column = jnp.sum(total, axis=1, keepdims=True)
    line = jnp.sum(jnp.where(row8 == lane8, column, 0.0), axis=0, keepdims=True)
    out[0] = line[:, 0:K]
    for copy in sends:
        copy.wait_send()


def per_device(mesh_shape, centers, box_radii, labels, certified, conv_weights, conv_bias,
               head_weight, head_bias):
    n_seg, n_rep, n_box = (mesh_shape[a] for a in ("segment", "rep", "box"))
    h = conv_weights.shape[-1]
    classes = head_bias.shape[0]
    dma = pltpu.SemaphoreType.DMA
    vmem = pl.BlockSpec(memory_space=pltpu.VMEM)
    hbm = pl.BlockSpec(memory_space=pl.ANY)
    return pl.pallas_call(
        functools.partial(kernel, n_seg, n_rep, n_box, classes),
        out_shape=jax.ShapeDtypeStruct((1, 1, K), f32),
        in_specs=[hbm] * 8,
        out_specs=vmem,
        scratch_shapes=[
            pltpu.SMEM(certified.shape, jnp.int32),
            pltpu.SMEM(labels.shape, jnp.int32),
            pltpu.VMEM(conv_bias.shape, f32),
            pltpu.VMEM((classes, h), bf16),
            pltpu.VMEM((1, classes), f32),
            pltpu.VMEM((TAPS, h, h), bf16),
            pltpu.VMEM((TAPS, 80, 128), bf16),
            pltpu.VMEM((TAPS, 80, h), bf16),
            pltpu.VMEM((128, h), bf16),
            pltpu.VMEM((8, 4, 4, h), f32),
            pltpu.VMEM((8, 4, 4, h), f32),
            pltpu.VMEM((2, 8, 128), f32),
            pltpu.VMEM((64, h), f32),
            pltpu.VMEM((2, 64, h // 2), bf16),
            pltpu.VMEM((2, 64, h // 2), bf16),
            pltpu.VMEM((2, 2, 80, h // 2), bf16),
            pltpu.VMEM((2, 2, 80, h // 2), bf16),
            pltpu.VMEM((2, 80, h), f32),
            pltpu.VMEM((2, 80, h), f32),
            pltpu.VMEM((2, 64, h // 2), f32),
            pltpu.VMEM((2, 16, h), f32),
            pltpu.VMEM((2, 16, h), f32),
            pltpu.VMEM((2, 8, h), f32),
            pltpu.VMEM((16, 128), f32),
            pltpu.VMEM((2 * n_seg, 16, 128), f32),
            dma((8,)),
            dma((len(TREE),)),
            dma((len(TREE),)),
            dma((len(TREE), 4)),
            dma((len(TREE), 4)),
            dma((len(TREE), 2)),
            dma((len(TREE), 2)),
            dma((3,)),
            dma((3,)),
            dma((2,)),
            dma((2,)),
            dma((2, 2)),
            dma((2, 2)),
            dma((2 * n_seg,)),
            dma((2 * n_seg,)),
        ],
        compiler_params=pltpu.CompilerParams(collective_id=0, has_side_effects=True),
    )(certified, labels, centers, box_radii, conv_weights, conv_bias, head_weight.T,
      head_bias[None, :])


def solution(mesh):
    placed = (
        P(("rep", "box"), None, None, None),
        P(("rep", "box"), None, None, None),
        P(("rep", "box")),
        P(("rep", "box")),
        P("segment", None, "box", None),
        P("segment", None),
        P(),
        P(),
    )
    return jax.shard_map(
        functools.partial(per_device, dict(mesh.shape)),
        mesh=mesh,
        in_specs=placed,
        out_specs=P(("rep", "box"), "segment", None),
        check_vma=False,
    )
```

```python
import functools

import jax
import jax.numpy as jnp
from jax import lax
from jax.experimental import pallas as pl
from jax.experimental.pallas import tpu as pltpu
from jax.sharding import PartitionSpec as P

K = 5
TAPS = 9
TREE = ((2,0),(-2,0),(4,2),(-4,-2),(3,2),(-3,-2),(6,4),(-6,-4),(5,4),(-5,-4),(8,6),(7,6),(-7,-6),(1,0),(-1,0))
FIRST = (2,-2,1,-1)
WHOLE = (1, -1)
LAG = 5
LAG2 = 9
bf16 = jnp.bfloat16
f32 = jnp.float32
MESH = pl.DeviceIdType.MESH


def kernel(
    n_seg, n_rep, n_box, classes,
    cert_in, lab_in, cen, rad, cw, bias_in, hw_in, hb_in, out,
    cert, lab, bias, hw, hb, W, S, L, G, C8, R8, PT, MID, fin, fout, cin, cout, CF, NEW, ACC, slope, cept, HC, HO, T,
    loc, zs, zr, ys, yr, cs, cr, xs, xr, fs, fr, bs, br, ts, tr,
):
    s = lax.axis_index("segment")
    r = lax.axis_index("rep")
    z = lax.axis_index("box")
    c = lax.rem(r, 2)
    mate = {"rep": r + 1 - 2 * c}
    y_up = {"rep": lax.rem(r + 2, n_rep)}
    y_down = {"rep": lax.rem(r + n_rep - 2, n_rep)}
    jumps = sorted({o - p for o, p in TREE} | {p - o for o, p in TREE})

    def along(o):
        return {"box": lax.rem(z + n_box + o, n_box)}

    peers = []
    for dx in range(n_seg):
        for dc in range(2):
            if dx or dc:
                peers.append(
                    {"segment": lax.rem(s + dx, n_seg), "rep": r + dc * (1 - 2 * c)}
                )
    shard = W.shape[1] // n_box
    half = shard // 2
    rows_y = n_rep // 2
    y = r // 2
    wide = W.shape[2] // 2
    slim = W.shape[2] // rows_y
    mid_tap = TAPS // 2

    own = pltpu.make_async_copy(
        cw.at[0], W.at[:, pl.ds(pl.multiple_of(z * shard, shard), shard), :], loc.at[0]
    )
    own.start()
    own_c = pltpu.make_async_copy(cen, C8.at[pl.ds(4 * c, 4)], loc.at[1])
    own_c.start()
    own_r = pltpu.make_async_copy(rad, R8.at[pl.ds(4 * c, 4)], loc.at[2])
    own_r.start()
    small = []
    for n, (there, here) in enumerate(
        ((cert_in, cert), (lab_in, lab), (bias_in, bias), (hw_in, hw), (hb_in, hb))
    ):
        copy = pltpu.make_async_copy(there, here, loc.at[3 + n])
        copy.start()
        small.append(copy)

    barrier = pltpu.get_barrier_semaphore()
    near = [y_up, y_down] + [along(o) for o in jumps] + peers
    for device in near:
        pl.semaphore_signal(barrier, inc=1, device_id=device, device_id_type=MESH)
    pl.semaphore_wait(barrier, len(near))

    def remote(src, dst, send, recv, device):
        return pltpu.make_async_remote_copy(
            src_ref=src, dst_ref=dst, send_sem=send, recv_sem=recv,
            device_id=device, device_id_type=MESH,
        )

    def piece(n, core, taps, lane, width, back=0):
        b = lax.rem(z + 2 * n_box - TREE[n][0] + back, n_box)
        row = pl.multiple_of(b * shard + core * half, half)
        lane = pl.multiple_of(lane, width) if width < 2 * wide else 0
        return W.at[pl.ds(taps[0], taps[1] - taps[0]), pl.ds(row, half), pl.ds(lane, width)]

    every, low_part, high_part = (0, TAPS), (0, mid_tap), (mid_tap, TAPS)
    y_next, y_prev = lax.rem(y + 1, rows_y), lax.rem(y + rows_y - 1, rows_y)
    y_far = lax.rem(y + 2, rows_y)

    def z_copy(n, arriving=False):
        offset, parent = TREE[n]
        back = 0 if arriving else offset - parent
        lane, width = (0, 2 * wide) if offset in WHOLE else (y * slim, slim)
        ref = piece(n, c, every, lane, width, back)
        return remote(ref, ref, zs.at[n], zr.at[n], along(offset - parent))

    def y_copies(n, arriving=False):
        out = []
        for d in () if TREE[n][0] in WHOLE else range(2):
            part = (y_prev, y_next)[d] if arriving else y
            ref = piece(n, c, every, part * slim, slim)
            out.append(remote(ref, ref, ys.at[n, d], yr.at[n, d], (y_up, y_down)[d]))
        return out

    def relay_copies(n, arriving=False):
        out = []
        for d in () if TREE[n][0] in WHOLE else range(2):
            part = y_far if arriving else (y_prev, y_next)[d]
            ref = piece(n, c, (low_part, high_part)[d], part * slim, slim)
            out.append(remote(ref, ref, ys.at[n, 2 + d], yr.at[n, 2 + d], (y_up, y_down)[d]))
        return out

    near_half = y // 2

    def c_copy(n, far, arriving=False):
        side = 1 - near_half if far else near_half
        ref = piece(n, 1 - c if arriving else c, every, side * wide, wide)
        return remote(ref, ref, cs.at[n, far], cr.at[n, far], mate)

    own.wait()
    index = {offset: n for n, (offset, _) in enumerate(TREE)}
    for offset in FIRST:
        z_copy(index[offset]).start()

    own_c.wait()
    own_r.wait()
    for copy in small:
        copy.wait()
    pair_c = remote(C8.at[pl.ds(4 * c, 4)], C8.at[pl.ds(4 * c, 4)], xs.at[0], xr.at[0], mate)
    pair_r = remote(R8.at[pl.ds(4 * c, 4)], R8.at[pl.ds(4 * c, 4)], xs.at[1], xr.at[1], mate)
    row8 = lax.broadcasted_iota(jnp.int32, (8, 128), 0)
    lane8 = lax.broadcasted_iota(jnp.int32, (8, 128), 1)
    tile = jnp.zeros((8, 128), f32)
    for i in range(4):
        alive_i = (1 - cert[i]).astype(f32)
        label_i = lab[i].astype(f32)
        here = lane8 == 4 * c + i
        tile = jnp.where(here & (row8 == 0), alive_i, tile)
        tile = jnp.where(here & (row8 == 1), label_i, tile)
    PT[c] = tile
    pair_t = remote(PT.at[c], PT.at[c], xs.at[2], xr.at[2], mate)
    pair_t.start()
    pair_c.start()
    pair_r.start()

    p_row = lax.broadcasted_iota(jnp.int32, (80, 128), 0)
    p_col = lax.broadcasted_iota(jnp.int32, (80, 128), 1)
    same = (p_row // 16) == (p_col // 16)
    dy = lax.rem(p_col, 16) // 4 - lax.rem(p_row, 16) // 4
    dx_ = lax.rem(p_col, 4) - lax.rem(p_row, 4)
    for t in range(TAPS):
        a, b = divmod(t, 3)
        S[t] = jnp.where(same & (dy == a - 1) & (dx_ == b - 1), 1.0, 0.0).astype(bf16)
    G[...] = jnp.zeros_like(G)

    count = len(TREE)

    def take_relayed(n):
        for copy in relay_copies(n, True):
            copy.wait_recv()
        if TREE[n][0] not in WHOLE:
            c_copy(n, 1).start()

    for n in range(count + LAG):
        if n < count:
            z_copy(n, True).wait_recv()
            for child, (_, parent) in enumerate(TREE):
                if parent == TREE[n][0]:
                    z_copy(child).start()
            for copy in y_copies(n):
                copy.start()
            if TREE[n][0] in WHOLE:
                for far in range(2):
                    c_copy(n, far).start()
        if n >= LAG:
            for copy in y_copies(n - LAG, True):
                copy.wait_recv()
            for copy in relay_copies(n - LAG):
                copy.start()
            if TREE[n - LAG][0] not in WHOLE:
                c_copy(n - LAG, 0).start()
        if n >= LAG2:
            take_relayed(n - LAG2)

    remote(PT.at[1 - c], PT.at[1 - c], xs.at[2], xr.at[2], mate).wait_recv()
    other = pl.ds(4 * (1 - c), 4)
    remote(C8.at[other], C8.at[other], xs.at[0], xr.at[0], mate).wait_recv()
    remote(R8.at[other], R8.at[other], xs.at[1], xr.at[1], mate).wait_recv()
    both = PT[0] + PT[1]
    alive_row = both[0:1, :]
    label_row = both[1:2, :]
    alive = jnp.sum(jnp.where(lane8 == row8, alive_row, 0.0), axis=1, keepdims=True)
    labels = jnp.sum(jnp.where(lane8 == row8, label_row, 0.0), axis=1, keepdims=True)
    rank = jnp.sum(jnp.where(lane8 < row8, alive_row, 0.0), axis=1, keepdims=True)
    live_no = jnp.where(alive > 0.5, rank, -1.0)
    first = (2 * c).astype(f32)

    @pl.when(s == 0)
    def _():
        for m in range(2):
            pick = jnp.where(live_no == first + m, 1.0, 0.0)
            middle = jnp.zeros((16, C8.shape[3]), f32)
            radius = jnp.zeros((16, C8.shape[3]), f32)
            for i in range(8):
                take = pick[i : i + 1, :] > 0.5
                middle = jnp.where(take, C8[i].reshape(middle.shape), middle)
                radius = jnp.where(take, R8[i].reshape(radius.shape), radius)
            MID[16 * m : 16 * m + 16] = middle
            MID[32 + 16 * m : 48 + 16 * m] = radius

    @pl.when(s == n_seg - 1)
    def _():
        row = lax.broadcasted_iota(jnp.int32, (16, 1), 0)
        spec = lax.rem(row, 8).astype(f32)
        lab0 = jnp.sum(jnp.where(live_no == first, labels, 0.0), axis=0, keepdims=True)
        lab1 = jnp.sum(jnp.where(live_no == first + 1.0, labels, 0.0), axis=0, keepdims=True)
        true = jnp.where(row < 8, lab0, lab1)
        rival = true + 1.0 + spec
        rival = jnp.where(rival >= classes, rival - classes, rival)
        ids = lax.broadcasted_iota(jnp.int32, (16, classes), 1).astype(f32)
        selector = jnp.where(ids == true, 1.0, 0.0) - jnp.where(ids == rival, 1.0, 0.0)
        selector = jnp.where(spec < K, selector, 0.0)
        pooled = lax.dot_general(
            selector.astype(bf16), hw[...], (((1,), (0,)), ((), ())), preferred_element_type=f32
        ) / 16.0
        HC[...] = pooled.reshape(2, 8, pooled.shape[1])
        offset = jnp.sum(selector * hb[...], axis=1, keepdims=True)
        lane16 = lax.broadcasted_iota(jnp.int32, (16, 128), 1)
        HO[...] = jnp.where(lane16 == 0, offset, 0.0)

    up_x = {"segment": lax.rem(s + 1, n_seg)}
    down_x = {"segment": lax.rem(s + n_seg - 1, n_seg)}
    part_h = W.shape[1] // 2
    cols = [slice(h * part_h, (h + 1) * part_h) for h in range(2)]
    rows_in = (((1,), (1,)), ((), ()))

    def f_copy(h):
        return remote(fout.at[h], fin.at[h], fs.at[h], fr.at[h], up_x)

    def b_copy(m, h):
        return remote(cout.at[m, h], cin.at[m, h], bs.at[m, h], br.at[m, h], down_x)

    def windows(h):
        here = pl.ds(pl.multiple_of(h * part_h, part_h), part_h)
        G[0:64, here] = MID[:, here].astype(bf16)
        for t in range(TAPS):
            L[t, 0:64, here] = jnp.dot(
                S[t, 0:64], G[:, here], preferred_element_type=f32
            ).astype(bf16)

    def half_forward(h, finish):
        here = pl.ds(pl.multiple_of(h * part_h, part_h), part_h)
        for n in range(2):
            start = ACC[n] if finish else jnp.zeros((64, part_h), f32)
            centre, spread = start[0:32], start[32:64]
            for t in range(TAPS):
                w = W[t, cols[n], here]
                centre += lax.dot_general(
                    L[t, 0:32, here], w, rows_in, preferred_element_type=f32
                )
                spread += lax.dot_general(
                    L[t, 32:64, here], jnp.abs(w), rows_in, preferred_element_type=f32
                )
            if not finish:
                ACC[n, 0:32] = centre
                ACC[n, 32:64] = spread
                continue
            centre = centre + bias[:, cols[n]]
            low = centre - spread
            up = centre + spread
            up_pos = jnp.maximum(up, 0.0)
            low_pos = jnp.maximum(low, 0.0)
            low_neg = jnp.maximum(-low, 0.0)
            fout[n, 0:32] = (MID[0:32, cols[n]] + 0.5 * (up_pos + low_pos)).astype(bf16)
            fout[n, 32:64] = (MID[32:64, cols[n]] + 0.5 * (up_pos - low_pos)).astype(bf16)

            @pl.when(s < n_seg - 1)
            def _():
                f_copy(n).start()

            slope_now = up_pos / (up_pos + low_neg)
            cept_now = slope_now * low_neg
            for m in range(2):
                slope[m, :, cols[n]] = slope_now[16 * m : 16 * m + 16]
                cept[m, :, cols[n]] = cept_now[16 * m : 16 * m + 16]

    for n in range(count):
        c_copy(n, 0, True).wait_recv()

    @pl.when(s == 0)
    def _():
        windows(near_half)
        half_forward(near_half, False)
        windows(1 - near_half)

    for n in range(count + LAG - LAG2, count):
        take_relayed(n)
    for n in range(count):
        c_copy(n, 1, True).wait_recv()

    @pl.when(s > 0)
    def _():
        f_copy(0).wait_recv()
        MID[:, cols[0]] = fin[0].astype(f32)
        windows(0)
        half_forward(0, False)
        f_copy(1).wait_recv()
        MID[:, cols[1]] = fin[1].astype(f32)
        windows(1)

    half_forward(jnp.where(s == 0, 1 - near_half, 1), True)

    slot = s * 2 + c

    def terms(m):
        for k in range(K):
            rows = slice(16 * k, 16 * k + 16)
            now = CF[m, rows]
            part = now * slope[m] * bias[...] + jnp.minimum(now, 0.0) * cept[m]
            new_k = NEW[m, rows]
            ends = new_k * MID[16 * m : 16 * m + 16] - jnp.abs(new_k) * MID[
                32 + 16 * m : 48 + 16 * m
            ]
            part = part + jnp.where(s == 0, ends, 0.0)
            part = jnp.sum(part, axis=0, keepdims=True)
            folded = part[:, 0:128]
            for q in range(1, part.shape[1] // 128):
                folded = folded + part[:, 128 * q : 128 * q + 128]
            at = 8 * m + k
            folded = folded + jnp.where(s == n_seg - 1, HO[at : at + 1, :], 0.0)
            T[slot, at : at + 1, :] = folded

    for m in range(2):
        for h in range(2):
            @pl.when(s == n_seg - 1)
            def _():
                for k in range(K):
                    CF[m, 16 * k : 16 * k + 16, cols[h]] = jnp.broadcast_to(
                        HC[m, k : k + 1, cols[h]], (16, part_h)
                    )

            @pl.when(s < n_seg - 1)
            def _():
                b_copy(m, h).wait_recv()
                CF[m, :, cols[h]] = cin[m, h].astype(f32)

            slope_m = slope[m, :, cols[h]]
            for k in range(K):
                rows = slice(16 * k, 16 * k + 16)
                G[rows, cols[h]] = (CF[m, rows, cols[h]] * slope_m).astype(bf16)
            for t in range(TAPS):
                L[t, :, cols[h]] = jnp.dot(
                    S[TAPS - 1 - t], G[:, cols[h]], preferred_element_type=f32
                ).astype(bf16)
            for n in range(2):
                new = NEW[m, :, cols[n]] if h else jnp.zeros((80, part_h), f32)
                for t in range(TAPS):
                    new += jnp.dot(
                        L[t, :, cols[h]], W[t, cols[h], cols[n]], preferred_element_type=f32
                    )
                if h == 0:
                    NEW[m, :, cols[n]] = new
                    continue
                new = new + CF[m, :, cols[n]]
                NEW[m, :, cols[n]] = new

                @pl.when(s > 0)
                def _():
                    cout[m, n] = new.astype(bf16)
                    b_copy(m, n).start()

        if m == 0:
            pl.when(s == 0)(functools.partial(terms, 0))

    pl.when(s > 0)(functools.partial(terms, 0))
    terms(1)

    sends = []
    for n, device in enumerate(peers):
        copy = remote(T.at[slot], T.at[slot], ts.at[n], tr.at[slot], device)
        copy.start()
        sends.append(copy)
    for n in range(count):
        for copy in [z_copy(n)] + y_copies(n) + relay_copies(n):
            copy.wait_send()
        for far in range(2):
            c_copy(n, far).wait_send()
    pair_c.wait_send()
    pair_r.wait_send()
    pair_t.wait_send()

    @pl.when(s < n_seg - 1)
    def _():
        for h in range(2):
            f_copy(h).wait_send()

    @pl.when(s > 0)
    def _():
        for m in range(2):
            for h in range(2):
                b_copy(m, h).wait_send()

    for dx in range(n_seg):
        for dc in range(2):
            if dx or dc:
                there = lax.rem(s + dx, n_seg) * 2 + c + dc * (1 - 2 * c)
                remote(T.at[there], T.at[there], ts.at[0], tr.at[there], mate).wait_recv()
    mine = jnp.where(row8[:, 0:1] == 4 * c + s, live_no, -1.0)
    mine = jnp.max(mine, axis=0, keepdims=True)
    total = jnp.zeros((8, 128), f32)
    for core in range(2):
        for m in range(2):
            part = T[core, 8 * m : 8 * m + 8]
            for x in range(1, n_seg):
                part = part + T[2 * x + core, 8 * m : 8 * m + 8]
            total = jnp.where((mine == float(2 * core + m)) & (row8 < K), part, total)
    column = jnp.sum(total, axis=1, keepdims=True)
    line = jnp.sum(jnp.where(row8 == lane8, column, 0.0), axis=0, keepdims=True)
    out[0] = line[:, 0:K]
    for copy in sends:
        copy.wait_send()


def per_device(mesh_shape, centers, box_radii, labels, certified, conv_weights, conv_bias,
               head_weight, head_bias):
    n_seg, n_rep, n_box = (mesh_shape[a] for a in ("segment", "rep", "box"))
    h = conv_weights.shape[-1]
    classes = head_bias.shape[0]
    dma = pltpu.SemaphoreType.DMA
    vmem = pl.BlockSpec(memory_space=pltpu.VMEM)
    hbm = pl.BlockSpec(memory_space=pl.ANY)
    return pl.pallas_call(
        functools.partial(kernel, n_seg, n_rep, n_box, classes),
        out_shape=jax.ShapeDtypeStruct((1, 1, K), f32),
        in_specs=[hbm] * 8,
        out_specs=vmem,
        scratch_shapes=[
            pltpu.SMEM(certified.shape, jnp.int32),
            pltpu.SMEM(labels.shape, jnp.int32),
            pltpu.VMEM(conv_bias.shape, f32),
            pltpu.VMEM((classes, h), bf16),
            pltpu.VMEM((1, classes), f32),
            pltpu.VMEM((TAPS, h, h), bf16),
            pltpu.VMEM((TAPS, 80, 128), bf16),
            pltpu.VMEM((TAPS, 80, h), bf16),
            pltpu.VMEM((128, h), bf16),
            pltpu.VMEM((8, 4, 4, h), f32),
            pltpu.VMEM((8, 4, 4, h), f32),
            pltpu.VMEM((2, 8, 128), f32),
            pltpu.VMEM((64, h), f32),
            pltpu.VMEM((2, 64, h // 2), bf16),
            pltpu.VMEM((2, 64, h // 2), bf16),
            pltpu.VMEM((2, 2, 80, h // 2), bf16),
            pltpu.VMEM((2, 2, 80, h // 2), bf16),
            pltpu.VMEM((2, 80, h), f32),
            pltpu.VMEM((2, 80, h), f32),
            pltpu.VMEM((2, 64, h // 2), f32),
            pltpu.VMEM((2, 16, h), f32),
            pltpu.VMEM((2, 16, h), f32),
            pltpu.VMEM((2, 8, h), f32),
            pltpu.VMEM((16, 128), f32),
            pltpu.VMEM((2 * n_seg, 16, 128), f32),
            dma((8,)),
            dma((len(TREE),)),
            dma((len(TREE),)),
            dma((len(TREE), 4)),
            dma((len(TREE), 4)),
            dma((len(TREE), 2)),
            dma((len(TREE), 2)),
            dma((3,)),
            dma((3,)),
            dma((2,)),
            dma((2,)),
            dma((2, 2)),
            dma((2, 2)),
            dma((2 * n_seg,)),
            dma((2 * n_seg,)),
        ],
        compiler_params=pltpu.CompilerParams(collective_id=0, has_side_effects=True),
    )(certified, labels, centers, box_radii, conv_weights, conv_bias, head_weight.T,
      head_bias[None, :])


def solution(mesh):
    placed = (
        P(("rep", "box"), None, None, None),
        P(("rep", "box"), None, None, None),
        P(("rep", "box")),
        P(("rep", "box")),
        P("segment", None, "box", None),
        P("segment", None),
        P(),
        P(),
    )
    return jax.shard_map(
        functools.partial(per_device, dict(mesh.shape)),
        mesh=mesh,
        in_specs=placed,
        out_specs=P(("rep", "box"), "segment", None),
        check_vma=False,
    )
```
